512 devices in a mesh: ctx: 16 (over z_hi, x), tp: 8 (over y), dp: 4 (over z_lo, core).
Axes of the slice: x: 4, y: 8, z: 8 (z_hi: 4, z_lo: 2; z = z_hi * 2 + z_lo), core: 2. Of those that a mesh axis runs over, the one named last changes fastest.
Arguments:
- q_raw: bfloat16 [4, 2048, 2048], P('dp', 'ctx', 'tp'), may hold values from -60 to 60
- k_raw: bfloat16 [4, 2048, 2048], P('dp', 'ctx', 'tp'), may hold values from -60 to 60
- value: bfloat16 [4, 2048, 2048], P('dp', 'ctx', 'tp'), may hold values from -6 to 6
- d_out: bfloat16 [4, 2048, 2048], P('dp', 'ctx', 'tp'), may hold values from -6 to 6
- q_gain: float32 [128], replicated, may hold values from 1.3 to 5
- k_gain: float32 [128], replicated, may hold values from 1.3 to 5
Outputs:
- q_raw_grad: bfloat16 [4, 2048, 2048], P('dp', 'ctx', 'tp')
- k_raw_grad: bfloat16 [4, 2048, 2048], P('dp', 'ctx', 'tp')
- value_grad: bfloat16 [4, 2048, 2048], P('dp', 'ctx', 'tp')
- q_gain_grad: float32 [128], replicated
- k_gain_grad: float32 [128], replicated
The draws below stay inside these ranges and needn't reach their ends.
All inputs are finite; a program needn't handle non-finite values.
Results may differ from the reference program's by a relative error of at most 0.028.
The reference program's roundings to bfloat16 on the way count: a program that leaves them out, or rounds other values in their place, can miss the bound.
Values may be sent and summed in bfloat16 or wider, within the bound.
A program may use at most 64 MiB of HBM per device.

```python
import math
import jax
import jax.numpy as jnp
from jax import lax

HEADS = 16
DH = 128
TOK_DEV = 128
CLIPS = 4
LENGTH = 2048
N_CTX = 16


def raw_pair(key):
    streams = jax.random.split(jax.random.fold_in(key, 7), 6)
    shape = (CLIPS, LENGTH, HEADS, DH)
    upper = math.log(10.0)
    base_q = jax.random.truncated_normal(streams[0], -4.0, 4.0, shape, jnp.float32)
    base_k = jax.random.truncated_normal(streams[1], -4.0, 4.0, shape, jnp.float32)
    row_q = jnp.exp(jax.random.uniform(streams[2], (CLIPS, LENGTH, HEADS, 1), jnp.float32, 0.0, upper))
    row_k = jnp.exp(jax.random.uniform(streams[3], (CLIPS, LENGTH, HEADS, 1), jnp.float32, 0.0, upper))
    col_q = jnp.exp(jax.random.uniform(streams[4], (1, 1, HEADS, DH), jnp.float32, 0.0, upper))
    col_k = jnp.exp(jax.random.uniform(streams[5], (1, 1, HEADS, DH), jnp.float32, 0.0, upper))
    query = base_q * row_q * col_q * 0.25
    keyed = base_k * row_k * col_k * 0.25
    query = jnp.clip(query, -60.0, 60.0).reshape(CLIPS, LENGTH, HEADS * DH)
    keyed = jnp.clip(keyed, -60.0, 60.0).reshape(CLIPS, LENGTH, HEADS * DH)
    return (query, keyed)


def draw_q_raw(key, part):
    return raw_pair(key)[0].astype(jnp.bfloat16)


def draw_k_raw(key, part):
    return raw_pair(key)[1].astype(jnp.bfloat16)


def draw_q_gain(key, part):
    return jax.random.uniform(jax.random.fold_in(key, 11), (DH,), jnp.float32, 1.3, 2.3)


def draw_k_gain(key, part):
    return jax.random.uniform(jax.random.fold_in(key, 13), (DH,), jnp.float32, 1.3, 2.3)


def block_levels(stream_key, dims, cuts, low, high):
    level = 1.0
    for position, shards_of in cuts:
        steps = jax.random.uniform(jax.random.fold_in(jax.random.fold_in(stream_key, 6), position), (shards_of,), jnp.float32, low / len(cuts), high / len(cuts))
        level = level * jnp.repeat(jnp.exp(steps), dims[position] // shards_of).reshape((-1,) + (1,) * (len(dims) - 1 - position))
    return level


def scatter_about(key, shape, deviation, reach, cuts=(), kind=jnp.bfloat16):
    values = jax.random.normal(key, shape, jnp.float32) * deviation
    if len(cuts) > 0:
        values = block_levels(key, shape, cuts, -0.22, 0.18) * values
    return jnp.clip(values, min=-reach, max=reach).astype(kind)


def setup_inputs(seed: int = 0) -> dict:
    keys = jax.random.split(jax.random.key(seed), 7)
    return {
        "q_raw": draw_q_raw(jax.random.fold_in(keys[6], 71), 0),
        "k_raw": draw_k_raw(jax.random.fold_in(keys[6], 71), 0),
        "value": scatter_about(keys[2], (CLIPS, LENGTH, HEADS * DH), 1.0, 6.0, ((0, 4), (1, 16), (2, 8))),
        "d_out": scatter_about(keys[3], (CLIPS, LENGTH, HEADS * DH), 1.0, 6.0, ((0, 4), (1, 16), (2, 8))),
        "q_gain": draw_q_gain(jax.random.fold_in(keys[6], 71), 0),
        "k_gain": draw_k_gain(jax.random.fold_in(keys[6], 71), 0),
    }


EPSILON = 1e-06

def normalize(raw, gain):
    values = raw.astype(jnp.float32).reshape(CLIPS, LENGTH, HEADS, DH)
    inverse = lax.rsqrt(lax.optimization_barrier(jnp.mean(values * values, axis=3, keepdims=True)) + EPSILON)
    unit = values * inverse
    return (unit, inverse, (unit * gain).astype(jnp.bfloat16))

def restore(grad_normed, unit, inverse, gain):
    scaled = grad_normed * gain
    back = inverse * (scaled - unit * lax.optimization_barrier(jnp.mean(scaled * unit, axis=3, keepdims=True)))
    gain_grad = lax.optimization_barrier(jnp.sum(grad_normed * unit, axis=(0, 1, 2))) / LENGTH
    return (back.astype(jnp.bfloat16).reshape(CLIPS, LENGTH, HEADS * DH), gain_grad)

def block_sum(left, right):
    leading_blocks = left.reshape(N_CTX, TOK_DEV, LENGTH).astype(jnp.float32)
    trailing_blocks = right.reshape(N_CTX, TOK_DEV, DH).astype(jnp.float32)
    portions = jnp.einsum('map,mat->mpt', leading_blocks, trailing_blocks)
    rounded = lax.optimization_barrier(portions.astype(jnp.bfloat16))
    return lax.optimization_barrier(jnp.sum(rounded.astype(jnp.float32), axis=0))

def head_grads(item):
    q_head, k_head, v_head, o_head = item
    scale = DH ** (-0.5)
    scores = jnp.dot(q_head, k_head.T, preferred_element_type=jnp.float32) * scale
    prob = jax.nn.softmax(scores, axis=1)
    dprob = jnp.dot(o_head, v_head.T, preferred_element_type=jnp.float32)
    delta = lax.optimization_barrier(jnp.sum(prob * dprob, axis=1, keepdims=True))
    prob_low = prob.astype(jnp.bfloat16)
    dscore = (prob * (dprob - delta) * scale).astype(jnp.bfloat16)
    query_head_gradient = jnp.dot(dscore, k_head, preferred_element_type=jnp.float32)
    return (query_head_gradient, block_sum(dscore, q_head), block_sum(prob_low, o_head))

def by_head(array):
    shaped = array.reshape(CLIPS, LENGTH, HEADS, DH)
    return jnp.transpose(shaped, (0, 2, 1, 3)).reshape(CLIPS * HEADS, LENGTH, DH)

def back_to_tokens(array):
    return jnp.transpose(array.reshape(CLIPS, HEADS, LENGTH, DH), (0, 2, 1, 3))

def reference(q_raw, k_raw, value, d_out, q_gain, k_gain):
    q_unit, q_inverse, q_normed = normalize(q_raw, q_gain)
    k_unit, k_inverse, k_normed = normalize(k_raw, k_gain)
    dq_all, dk_all, dv_all = lax.map(head_grads, (by_head(q_normed), by_head(k_normed), by_head(value), by_head(d_out)))
    q_grad, q_gain_grad = restore(back_to_tokens(dq_all), q_unit, q_inverse, q_gain)
    k_grad, k_gain_grad = restore(back_to_tokens(dk_all), k_unit, k_inverse, k_gain)
    value_grad = back_to_tokens(dv_all).reshape(CLIPS, LENGTH, HEADS * DH).astype(jnp.bfloat16)
    return (q_grad, k_grad, value_grad, q_gain_grad, k_gain_grad)
```

```python
import functools

import jax
import jax.numpy as jnp
from jax import lax
from jax.experimental import pallas as pl
from jax.experimental.pallas import tpu as pltpu
from jax.sharding import PartitionSpec as P

EPSILON = 1e-06
SIDE = 4
MESH = pl.DeviceIdType.MESH


def kernel(
    sizes,
    q_ref,
    k_ref,
    v_ref,
    o_ref,
    q_gain_ref,
    k_gain_ref,
    dq_out,
    dk_out,
    dv_out,
    gain_out,
    q_raw,
    k_raw,
    v_all,
    o_all,
    q_normed,
    q_unit,
    q_inverse,
    k_normed,
    k_unit,
    k_inverse,
    k_turned,
    expo,
    dprob,
    stat_own,
    stat_in,
    acc,
    dkv_send,
    dkv_in,
    dq_own,
    dq_send,
    dq_in,
    gain_dp,
    gain_x,
    gain_z,
    gain_tp,
    send_sem,
    recv_sem,
):
    n_tp, n_dp, heads, length = sizes
    rows = q_ref.shape[0]
    width = q_gain_ref.shape[1]
    keys = SIDE * rows
    flat = heads * width
    scale = width ** (-0.5)
    ctx = lax.axis_index("ctx")
    tp = lax.axis_index("tp")
    dp = lax.axis_index("dp")
    x = lax.rem(ctx, SIDE)
    z = ctx // SIDE

    def along_x(step):
        return {"ctx": z * SIDE + lax.rem(x + step, SIDE), "tp": tp, "dp": dp}

    def along_z(step):
        return {"ctx": lax.rem(z + step, SIDE) * SIDE + x, "tp": tp, "dp": dp}

    def along_dp(step):
        return {"ctx": ctx, "tp": tp, "dp": lax.rem(dp + step, n_dp)}

    def along_tp(step):
        return {"ctx": ctx, "tp": lax.rem(tp + step, n_tp), "dp": dp}

    count = [0]
    started = []

    def copy(src, dst, device):
        index = count[0]
        count[0] += 1
        one = pltpu.make_async_remote_copy(
            src_ref=src,
            dst_ref=dst,
            send_sem=send_sem.at[index],
            recv_sem=recv_sem.at[index],
            device_id=device,
            device_id_type=MESH,
        )
        started.append(one)
        return one

    def cols(head):
        return slice(head * width, (head + 1) * width)

    barrier = pltpu.get_barrier_semaphore()
    partners = (
        [along_x(step) for step in range(1, SIDE)]
        + [along_z(step) for step in range(1, SIDE)]
        + [along_dp(step) for step in range(1, n_dp)]
        + [along_tp(step) for step in range(1, n_tp)]
    )
    for partner in partners:
        pl.semaphore_signal(barrier, inc=1, device_id=partner, device_id_type=MESH)
    pl.semaphore_wait(barrier, len(partners))

    q_up = copy(q_ref, q_raw.at[1], along_z(1))
    q_down = copy(q_ref, q_raw.at[3], along_z(3))
    o_up = copy(o_ref, o_all.at[1], along_z(1))
    o_down = copy(o_ref, o_all.at[3], along_z(3))
    k_up = copy(k_ref, k_raw.at[1], along_x(1))
    k_down = copy(k_ref, k_raw.at[3], along_x(3))
    v_up = copy(v_ref, v_all.at[1], along_x(1))
    v_down = copy(v_ref, v_all.at[3], along_x(3))
    for one in (q_up, o_down, o_up, q_down, k_up, v_down, v_up, k_down):
        one.start()
    q_far = copy(q_raw.at[1], q_raw.at[2], along_z(1))
    o_far = copy(o_all.at[3], o_all.at[2], along_z(3))
    k_far = copy(k_raw.at[1], k_raw.at[2], along_x(1))
    v_far = copy(v_all.at[3], v_all.at[2], along_x(3))

    v_all[0] = v_ref[...]
    o_all[0] = o_ref[...]
    acc[...] = jnp.zeros_like(acc)
    stat_own[...] = jnp.zeros_like(stat_own)

    def norm_q(slot, raw):
        for head in range(heads):
            values = raw[:, cols(head)].astype(jnp.float32)
            inverse = lax.rsqrt(jnp.mean(values * values, axis=1, keepdims=True) + EPSILON)
            unit = values * inverse
            q_unit[slot, :, cols(head)] = unit
            q_normed[slot, :, cols(head)] = (unit * q_gain_ref[...]).astype(jnp.bfloat16)
            if slot == 0:
                q_inverse[:, cols(head)] = jnp.broadcast_to(inverse, (rows, width))

    def norm_k(slot, raw):
        here = slice(slot * rows, (slot + 1) * rows)
        for head in range(heads):
            values = raw[:, cols(head)].astype(jnp.float32)
            inverse = lax.rsqrt(jnp.mean(values * values, axis=1, keepdims=True) + EPSILON)
            unit = values * inverse
            normed = unit * k_gain_ref[...]
            k_unit[here, cols(head)] = unit
            k_normed[here, cols(head)] = normed.astype(jnp.bfloat16)
            k_turned[head, :, here] = normed.astype(jnp.bfloat16).T
            if slot == 0:
                k_inverse[:, cols(head)] = jnp.broadcast_to(inverse, (rows, width))

    norm_q(0, q_ref[...])
    norm_k(0, k_ref[...])

    k_up.wait_recv()
    k_far.start()
    v_down.wait_recv()
    v_far.start()
    norm_k(1, k_raw[1])
    k_down.wait_recv()
    norm_k(3, k_raw[3])
    q_up.wait_recv()
    q_far.start()
    o_down.wait_recv()
    o_far.start()
    k_far.wait_recv()
    norm_k(2, k_raw[2])
    v_up.wait_recv()
    v_far.wait_recv()

    def contract_last(left, right):
        return lax.dot_general(
            left, right, (((1,), (1,)), ((), ())), preferred_element_type=jnp.float32
        )

    stat_copies = {}

    def first_pass(slot):
        for head in range(heads):
            scores = (
                contract_last(k_normed[:, cols(head)], q_normed[slot, :, cols(head)]) * scale
            )
            top = jnp.max(scores, axis=0, keepdims=True)
            weights = jnp.exp(scores - top)
            slopes = contract_last(
                v_all[:, :, cols(head)].reshape(keys, width), o_all[slot, :, cols(head)]
            )
            expo[slot, head] = weights
            dprob[slot, head] = slopes
            stat_own[slot, 3 * head : 3 * head + 1] = top
            stat_own[slot, 3 * head + 1 : 3 * head + 2] = jnp.sum(weights, axis=0, keepdims=True)
            stat_own[slot, 3 * head + 2 : 3 * head + 3] = jnp.sum(
                weights * slopes, axis=0, keepdims=True
            )
        for step in range(1, SIDE):
            there = (slot + step) % SIDE
            one = copy(stat_own.at[slot], stat_in.at[there, step], along_z(step))
            stat_copies[there, step] = one
            one.start()

    first_pass(0)
    o_up.wait_recv()
    norm_q(1, q_raw[1])
    first_pass(1)
    q_down.wait_recv()
    norm_q(3, q_raw[3])
    first_pass(3)
    q_far.wait_recv()
    norm_q(2, q_raw[2])
    o_far.wait_recv()
    first_pass(2)

    dq_copies = []
    q_gain_part = jnp.zeros((1, width), jnp.float32)

    def second_pass(slot):
        for step in range(1, SIDE):
            stat_copies[slot, step].wait_recv()
        part = jnp.zeros((1, width), jnp.float32)
        for head in range(heads):
            tops = [stat_own[slot, 3 * head : 3 * head + 1]]
            totals = [stat_own[slot, 3 * head + 1 : 3 * head + 2]]
            weighted = [stat_own[slot, 3 * head + 2 : 3 * head + 3]]
            for step in range(1, SIDE):
                tops.append(stat_in[slot, step, 3 * head : 3 * head + 1])
                totals.append(stat_in[slot, step, 3 * head + 1 : 3 * head + 2])
                weighted.append(stat_in[slot, step, 3 * head + 2 : 3 * head + 3])
            top = functools.reduce(jnp.maximum, tops)
            factors = [jnp.exp(one - top) for one in tops]
            total = sum(one * factor for one, factor in zip(totals, factors))
            delta = sum(one * factor for one, factor in zip(weighted, factors)) / total
            prob = expo[slot, head] * (factors[0] / total)
            dscore = (prob * (dprob[slot, head] - delta) * scale).astype(jnp.bfloat16)
            prob_low = prob.astype(jnp.bfloat16)
            turned = jnp.dot(k_turned[head], dscore, preferred_element_type=jnp.float32)
            dq = turned.T
            part += jnp.sum(dq * q_unit[slot, :, cols(head)], axis=0, keepdims=True)
            if slot == 0:
                dq_own[:, cols(head)] = dq
            else:
                dq_send[slot, :, cols(head)] = dq.astype(jnp.bfloat16)
            acc[:, cols(head)] += jnp.dot(
                dscore, q_normed[slot, :, cols(head)], preferred_element_type=jnp.float32
            )
            acc[:, flat + head * width : flat + (head + 1) * width] += jnp.dot(
                prob_low, o_all[slot, :, cols(head)], preferred_element_type=jnp.float32
            )
        if slot > 0:
            one = copy(dq_send.at[slot], dq_in.at[slot], along_z(SIDE - slot))
            dq_copies.append(one)
            one.start()
        return part

    for slot in (1, 3, 0, 2):
        q_gain_part += second_pass(slot)

    dkv_copies = []
    for slot in (2, 1, 3):
        here = slice(slot * rows, (slot + 1) * rows)
        dkv_send[slot] = acc[here, :].astype(jnp.bfloat16)
        one = copy(dkv_send.at[slot], dkv_in.at[slot], along_x(SIDE - slot))
        dkv_copies.append(one)
        one.start()
    k_gain_part = jnp.zeros((1, width), jnp.float32)
    for head in range(heads):
        k_gain_part += jnp.sum(acc[:, cols(head)] * k_unit[:, cols(head)], axis=0, keepdims=True)

    line = lax.broadcasted_iota(jnp.int32, (8, width), 0)
    part = jnp.where(line == 0, q_gain_part, jnp.where(line == 1, k_gain_part, 0.0))

    def restore(grad, unit, inverse, gain):
        scaled = grad * gain
        return inverse * (scaled - unit * jnp.mean(scaled * unit, axis=1, keepdims=True))

    def finish_q():
        for one in dq_copies:
            one.wait_recv()
        for head in range(heads):
            grad = dq_own[:, cols(head)]
            for slot in range(1, SIDE):
                grad += dq_in[slot, :, cols(head)].astype(jnp.float32)
            dq_out[:, cols(head)] = restore(
                grad, q_unit[0, :, cols(head)], q_inverse[:, cols(head)], q_gain_ref[...]
            ).astype(jnp.bfloat16)

    def finish_k():
        for one in dkv_copies:
            one.wait_recv()
        for head in range(heads):
            there = slice(flat + head * width, flat + (head + 1) * width)
            grad = acc[:rows, cols(head)]
            total = acc[:rows, there]
            for slot in range(1, SIDE):
                grad += dkv_in[slot, :, cols(head)].astype(jnp.float32)
                total += dkv_in[slot, :, there].astype(jnp.float32)
            dk_out[:, cols(head)] = restore(
                grad, k_unit[:rows, cols(head)], k_inverse[:, cols(head)], k_gain_ref[...]
            ).astype(jnp.bfloat16)
            dv_out[:, cols(head)] = total.astype(jnp.bfloat16)

    stages = (
        (gain_dp, n_dp, dp, along_dp, None),
        (gain_x, SIDE, x, along_x, finish_q),
        (gain_z, SIDE, z, along_z, finish_k),
        (gain_tp, n_tp, tp, along_tp, None),
    )
    for buffer, size, place, device, between in stages:
        buffer[place] = part
        copies = []
        for step in range(1, size):
            one = copy(buffer.at[place], buffer.at[place], device(step))
            copies.append(one)
            one.start()
        if between is not None:
            between()
        for one in copies:
            one.wait_recv()
        part = buffer[0]
        for index in range(1, size):
            part += buffer[index]
    gain_out[...] = part / length
    for one in started:
        one.wait_send()


def local(q_raw, k_raw, value, d_out, q_gain, k_gain):
    width = q_gain.shape[0]
    rows, flat = q_raw.shape[1:]
    heads = flat // width
    n_ctx, n_tp, n_dp = (lax.axis_size(name) for name in ("ctx", "tp", "dp"))
    keys = SIDE * rows
    low, full = jnp.bfloat16, jnp.float32
    copies = 12 + 12 + 3 + 3 + 2 * (SIDE - 1) + n_dp - 1 + n_tp - 1
    sizes = (n_tp, n_dp, heads, n_ctx * rows)
    block = jax.ShapeDtypeStruct((rows, flat), low)
    vmem = pl.BlockSpec(memory_space=pltpu.VMEM)
    dq, dk, dv, gains = pl.pallas_call(
        functools.partial(kernel, sizes),
        out_shape=(block, block, block, jax.ShapeDtypeStruct((8, width), full)),
        in_specs=[vmem] * 6,
        out_specs=(vmem,) * 4,
        scratch_shapes=[
            pltpu.VMEM((SIDE, rows, flat), low),
            pltpu.VMEM((SIDE, rows, flat), low),
            pltpu.VMEM((SIDE, rows, flat), low),
            pltpu.VMEM((SIDE, rows, flat), low),
            pltpu.VMEM((SIDE, rows, flat), low),
            pltpu.VMEM((SIDE, rows, flat), full),
            pltpu.VMEM((rows, flat), full),
            pltpu.VMEM((keys, flat), low),
            pltpu.VMEM((keys, flat), full),
            pltpu.VMEM((rows, flat), full),
            pltpu.VMEM((heads, width, keys), low),
            pltpu.VMEM((SIDE, heads, keys, rows), full),
            pltpu.VMEM((SIDE, heads, keys, rows), full),
            pltpu.VMEM((SIDE, 8, rows), full),
            pltpu.VMEM((SIDE, SIDE, 8, rows), full),
            pltpu.VMEM((keys, 2 * flat), full),
            pltpu.VMEM((SIDE, rows, 2 * flat), low),
            pltpu.VMEM((SIDE, rows, 2 * flat), low),
            pltpu.VMEM((rows, flat), full),
            pltpu.VMEM((SIDE, rows, flat), low),
            pltpu.VMEM((SIDE, rows, flat), low),
            pltpu.VMEM((n_dp, 8, width), full),
            pltpu.VMEM((SIDE, 8, width), full),
            pltpu.VMEM((SIDE, 8, width), full),
            pltpu.VMEM((n_tp, 8, width), full),
            pltpu.SemaphoreType.DMA((copies,)),
            pltpu.SemaphoreType.DMA((copies,)),
        ],
        compiler_params=pltpu.CompilerParams(collective_id=0, has_side_effects=True),
    )(
        q_raw[0],
        k_raw[0],
        value[0],
        d_out[0],
        q_gain[None],
        k_gain[None],
    )
    return (dq[None], dk[None], dv[None], gains[0], gains[1])


def solution(mesh):
    split = P("dp", "ctx", "tp")
    return jax.shard_map(
        local,
        mesh=mesh,
        in_specs=(split, split, split, split, P(), P()),
        out_specs=(split, split, split, P(), P()),
        check_vma=False,
    )
```

```python
import functools

import jax
import jax.numpy as jnp
from jax import lax
from jax.experimental import pallas as pl
from jax.experimental.pallas import tpu as pltpu
from jax.sharding import PartitionSpec as P

EPSILON = 1e-06
SIDE = 4
MESH = pl.DeviceIdType.MESH


def kernel(
    sizes,
    q_hbm,
    k_hbm,
    v_hbm,
    o_hbm,
    q_gain_hbm,
    k_gain_hbm,
    dq_out,
    dk_out,
    dv_out,
    gain_out,
    q_gain_ref,
    k_gain_ref,
    q_raw,
    k_raw,
    v_all,
    o_all,
    q_normed,
    q_unit,
    q_inverse,
    k_normed,
    k_unit,
    k_inverse,
    k_turned,
    expo,
    dprob,
    stat_own,
    stat_in,
    dk_acc,
    dv_acc,
    dk_send,
    dv_send,
    dk_in,
    dv_in,
    dk_far,
    dv_far,
    dq_full,
    dq_send,
    dq_in,
    dq_far,
    gain_tp,
    gain_z,
    gain_x,
    load_sem,
    send_sem,
    recv_sem,
):
    n_tp, n_dp, heads, length = sizes
    rows = q_hbm.shape[0]
    width = q_gain_hbm.shape[1]
    keys = SIDE * rows
    scale = width ** (-0.5)
    ctx = lax.axis_index("ctx")
    tp = lax.axis_index("tp")
    dp = lax.axis_index("dp")
    x = lax.rem(ctx, SIDE)
    z = ctx // SIDE

    def along_x(step):
        return {"ctx": z * SIDE + lax.rem(x + step, SIDE), "tp": tp, "dp": dp}

    def along_z(step):
        return {"ctx": lax.rem(z + step, SIDE) * SIDE + x, "tp": tp, "dp": dp}

    def along_z_dp(step):
        place = lax.rem(z + step // n_dp, SIDE) * SIDE + x
        return {"ctx": place, "tp": tp, "dp": lax.rem(dp + step % n_dp, n_dp)}

    def along_tp(step):
        return {"ctx": ctx, "tp": lax.rem(tp + step, n_tp), "dp": dp}

    barrier = pltpu.get_barrier_semaphore()
    partners = (
        [along_z_dp(step) for step in range(1, SIDE * n_dp)]
        + [along_tp(step) for step in range(1, n_tp)]
        + [along_x(step) for step in range(1, SIDE)]
    )
    for partner in partners:
        pl.semaphore_signal(barrier, inc=1, device_id=partner, device_id_type=MESH)

    loads = [
        pltpu.make_async_copy(src, dst, load_sem.at[index])
        for index, (src, dst) in enumerate(
            (
                (q_gain_hbm, q_gain_ref),
                (k_gain_hbm, k_gain_ref),
                (k_hbm, k_raw.at[0]),
                (q_hbm, q_raw.at[0]),
                (v_hbm, v_all.at[0]),
                (o_hbm, o_all.at[0]),
            )
        )
    ]
    for one in loads:
        one.start()

    count = [0]
    started = []

    def copy(src, dst, device):
        index = count[0]
        count[0] += 1
        one = pltpu.make_async_remote_copy(
            src_ref=src,
            dst_ref=dst,
            send_sem=send_sem.at[index],
            recv_sem=recv_sem.at[index],
            device_id=device,
            device_id_type=MESH,
        )
        started.append(one)
        return one

    def cols(head):
        return slice(head * width, (head + 1) * width)

    pl.semaphore_wait(barrier, len(partners))

    q_up = copy(q_hbm, q_raw.at[1], along_z(1))
    q_down = copy(q_hbm, q_raw.at[3], along_z(3))
    o_up = copy(o_hbm, o_all.at[1], along_z(1))
    o_down = copy(o_hbm, o_all.at[3], along_z(3))
    k_up = copy(k_hbm, k_raw.at[1], along_x(1))
    k_down = copy(k_hbm, k_raw.at[3], along_x(3))
    v_up = copy(v_hbm, v_all.at[1], along_x(1))
    v_down = copy(v_hbm, v_all.at[3], along_x(3))
    for one in (q_up, o_down, k_up, v_down, o_up, q_down, v_up, k_down):
        one.start()
    q_far = copy(q_raw.at[1], q_raw.at[2], along_z(1))
    o_far = copy(o_all.at[3], o_all.at[2], along_z(3))
    k_far = copy(k_raw.at[1], k_raw.at[2], along_x(1))
    v_far = copy(v_all.at[3], v_all.at[2], along_x(3))

    dk_acc[...] = jnp.zeros_like(dk_acc)
    dv_acc[...] = jnp.zeros_like(dv_acc)
    stat_own[...] = jnp.zeros_like(stat_own)
    for one in loads:
        one.wait()

    def norm_q(slot):
        for head in range(heads):
            values = q_raw[slot, :, cols(head)].astype(jnp.float32)
            inverse = lax.rsqrt(jnp.mean(values * values, axis=1, keepdims=True) + EPSILON)
            unit = values * inverse
            q_unit[slot, :, cols(head)] = unit
            q_normed[slot, :, cols(head)] = (unit * q_gain_ref[...]).astype(jnp.bfloat16)
            if slot == 0:
                q_inverse[:, cols(head)] = jnp.broadcast_to(inverse, (rows, width))

    def norm_k(slot):
        here = slice(slot * rows, (slot + 1) * rows)
        for head in range(heads):
            values = k_raw[slot, :, cols(head)].astype(jnp.float32)
            inverse = lax.rsqrt(jnp.mean(values * values, axis=1, keepdims=True) + EPSILON)
            unit = values * inverse
            normed = (unit * k_gain_ref[...]).astype(jnp.bfloat16)
            k_unit[here, cols(head)] = unit
            k_normed[here, cols(head)] = normed
            k_turned[head, :, here] = normed.T
            if slot == 0:
                k_inverse[:, cols(head)] = jnp.broadcast_to(inverse, (rows, width))

    norm_q(0)
    norm_k(0)

    k_up.wait_recv()
    k_far.start()
    v_down.wait_recv()
    v_far.start()
    norm_k(1)
    k_down.wait_recv()
    norm_k(3)
    v_up.wait_recv()
    q_up.wait_recv()
    q_far.start()
    o_down.wait_recv()
    o_far.start()
    k_far.wait_recv()
    norm_k(2)
    v_far.wait_recv()

    def contract_last(left, right):
        return lax.dot_general(
            left, right, (((1,), (1,)), ((), ())), preferred_element_type=jnp.float32
        )

    stat_copies = {}

    def first_pass(slot):
        for head in range(heads):
            scores = (
                contract_last(k_normed[:, cols(head)], q_normed[slot, :, cols(head)]) * scale
            )
            top = jnp.max(scores, axis=0, keepdims=True)
            weights = jnp.exp(scores - top)
            slopes = contract_last(
                v_all[:, :, cols(head)].reshape(keys, width), o_all[slot, :, cols(head)]
            )
            expo[slot, head] = weights
            dprob[slot, head] = slopes
            stat_own[slot, 3 * head : 3 * head + 1] = top
            stat_own[slot, 3 * head + 1 : 3 * head + 2] = jnp.sum(weights, axis=0, keepdims=True)
            stat_own[slot, 3 * head + 2 : 3 * head + 3] = jnp.sum(
                weights * slopes, axis=0, keepdims=True
            )
        for step in (2, 1, 3):
            there = (slot + step) % SIDE
            one = copy(stat_own.at[slot], stat_in.at[there, step], along_z(step))
            stat_copies[there, step] = one
            one.start()

    first_pass(0)
    o_up.wait_recv()
    norm_q(1)
    first_pass(1)
    q_down.wait_recv()
    norm_q(3)
    first_pass(3)
    q_far.wait_recv()
    norm_q(2)
    o_far.wait_recv()
    first_pass(2)

    def second_pass(slot):
        for step in range(1, SIDE):
            stat_copies[slot, step].wait_recv()
        part = jnp.zeros((1, width), jnp.float32)
        for head in range(heads):
            tops = [stat_own[slot, 3 * head : 3 * head + 1]]
            totals = [stat_own[slot, 3 * head + 1 : 3 * head + 2]]
            weighted = [stat_own[slot, 3 * head + 2 : 3 * head + 3]]
            for step in range(1, SIDE):
                tops.append(stat_in[slot, step, 3 * head : 3 * head + 1])
                totals.append(stat_in[slot, step, 3 * head + 1 : 3 * head + 2])
                weighted.append(stat_in[slot, step, 3 * head + 2 : 3 * head + 3])
            top = functools.reduce(jnp.maximum, tops)
            factors = [jnp.exp(one - top) for one in tops]
            total = sum(one * factor for one, factor in zip(totals, factors))
            delta = sum(one * factor for one, factor in zip(weighted, factors)) / total
            prob = expo[slot, head] * (factors[0] / total)
            dscore = (prob * (dprob[slot, head] - delta) * scale).astype(jnp.bfloat16)
            prob_low = prob.astype(jnp.bfloat16)
            dq = jnp.dot(k_turned[head], dscore, preferred_element_type=jnp.float32).T
            part += jnp.sum(dq * q_unit[slot, :, cols(head)], axis=0, keepdims=True)
            dq_full[slot, head] = dq
            dk_acc[:, cols(head)] += jnp.dot(
                dscore, q_normed[slot, :, cols(head)], preferred_element_type=jnp.float32
            )
            dv_acc[:, cols(head)] += jnp.dot(
                prob_low, o_all[slot, :, cols(head)], preferred_element_type=jnp.float32
            )
        return part

    def via(head):
        return 1 if head % 2 == 0 else 3

    def start(src, dst, device):
        one = copy(src, dst, device)
        one.start()
        return one

    dq_far_copies, dq_copies = [], []
    q_gain_part = second_pass(2)
    for head in range(heads):
        dq_send[2, head] = dq_full[2, head].astype(jnp.bfloat16)
        device = along_z(SIDE - via(head))
        dq_far_copies.append(start(dq_send.at[2, head], dq_far.at[head], device))
    for slot in (1, 3):
        q_gain_part += second_pass(slot)
        for head in range(heads):
            if via(head) != slot:
                dq_send[slot, head] = dq_full[slot, head].astype(jnp.bfloat16)
                device = along_z(SIDE - slot)
                dq_copies.append(start(dq_send.at[slot, head], dq_in.at[slot, head], device))
    q_gain_part += second_pass(0)

    def block(slot):
        return slice(slot * rows, (slot + 1) * rows)

    dk_send[2] = dk_acc[block(2), :].astype(jnp.bfloat16)
    dk_far_copy = start(dk_send.at[2], dk_far, along_x(3))
    dv_send[2] = dv_acc[block(2), :].astype(jnp.bfloat16)
    dv_far_copy = start(dv_send.at[2], dv_far, along_x(1))
    dk_send[3] = dk_acc[block(3), :].astype(jnp.bfloat16)
    dk_near = start(dk_send.at[3], dk_in.at[3], along_x(1))
    dv_send[1] = dv_acc[block(1), :].astype(jnp.bfloat16)
    dv_near = start(dv_send.at[1], dv_in.at[1], along_x(3))

    k_gain_part = jnp.zeros((1, width), jnp.float32)
    for head in range(heads):
        k_gain_part += jnp.sum(
            dk_acc[:, cols(head)] * k_unit[:, cols(head)], axis=0, keepdims=True
        )
    line = lax.broadcasted_iota(jnp.int32, (8, width), 0)
    part = jnp.where(line == 0, q_gain_part, jnp.where(line == 1, k_gain_part, 0.0))

    def spread(buffer, size, place, device, part):
        buffer[place] = part
        return [
            start(buffer.at[place], buffer.at[place], device(step)) for step in range(1, size)
        ]

    def gathered(buffer, size, copies):
        for one in copies:
            one.wait_recv()
        part = buffer[0]
        for index in range(1, size):
            part += buffer[index]
        return part

    gain_copies = spread(gain_tp, n_tp, tp, along_tp, part)

    for head in range(heads):
        slot = via(head)
        dq_far_copies[head].wait_recv()
        total = dq_full[slot, head] + dq_far[head].astype(jnp.float32)
        dq_send[slot, head] = total.astype(jnp.bfloat16)
        device = along_z(SIDE - slot)
        dq_copies.append(start(dq_send.at[slot, head], dq_in.at[slot, head], device))

    dk_far_copy.wait_recv()
    total = dk_acc[block(1), :] + dk_far[...].astype(jnp.float32)
    dk_send[1] = total.astype(jnp.bfloat16)
    dk_last = start(dk_send.at[1], dk_in.at[1], along_x(3))
    dv_far_copy.wait_recv()
    total = dv_acc[block(3), :] + dv_far[...].astype(jnp.float32)
    dv_send[3] = total.astype(jnp.bfloat16)
    dv_last = start(dv_send.at[3], dv_in.at[3], along_x(1))

    part = gathered(gain_tp, n_tp, gain_copies)
    gain_copies = spread(gain_z, SIDE * n_dp, z * n_dp + dp, along_z_dp, part)

    def restore(grad, unit, inverse, gain):
        scaled = grad * gain
        return inverse * (scaled - unit * jnp.mean(scaled * unit, axis=1, keepdims=True))

    for one in dq_copies:
        one.wait_recv()
    for head in range(heads):
        grad = dq_full[0, head]
        for slot in (1, 3):
            grad += dq_in[slot, head].astype(jnp.float32)
        dq_out[:, cols(head)] = restore(
            grad, q_unit[0, :, cols(head)], q_inverse[:, cols(head)], q_gain_ref[...]
        ).astype(jnp.bfloat16)

    part = gathered(gain_z, SIDE * n_dp, gain_copies)
    gain_copies = spread(gain_x, SIDE, x, along_x, part)

    for one in (dk_near, dv_near, dk_last, dv_last):
        one.wait_recv()
    for head in range(heads):
        grad = dk_acc[block(0), cols(head)]
        total = dv_acc[block(0), cols(head)]
        for slot in (1, 3):
            grad += dk_in[slot, :, cols(head)].astype(jnp.float32)
            total += dv_in[slot, :, cols(head)].astype(jnp.float32)
        dk_out[:, cols(head)] = restore(
            grad, k_unit[block(0), cols(head)], k_inverse[:, cols(head)], k_gain_ref[...]
        ).astype(jnp.bfloat16)
        dv_out[:, cols(head)] = total.astype(jnp.bfloat16)

    gain_out[...] = gathered(gain_x, SIDE, gain_copies) / length
    for one in started:
        one.wait_send()


def local(q_raw, k_raw, value, d_out, q_gain, k_gain):
    width = q_gain.shape[0]
    rows, flat = q_raw.shape[1:]
    heads = flat // width
    n_ctx, n_tp, n_dp = (lax.axis_size(name) for name in ("ctx", "tp", "dp"))
    keys = SIDE * rows
    low, full = jnp.bfloat16, jnp.float32
    copies = 12 + 12 + 3 * heads + 6 + SIDE * n_dp - 1 + n_tp - 1 + SIDE - 1
    sizes = (n_tp, n_dp, heads, n_ctx * rows)
    block = jax.ShapeDtypeStruct((rows, flat), low)
    vmem = pl.BlockSpec(memory_space=pltpu.VMEM)
    dq, dk, dv, gains = pl.pallas_call(
        functools.partial(kernel, sizes),
        out_shape=(block, block, block, jax.ShapeDtypeStruct((8, width), full)),
        in_specs=[pl.BlockSpec(memory_space=pl.ANY)] * 6,
        out_specs=(vmem,) * 4,
        scratch_shapes=[
            pltpu.VMEM((1, width), full),
            pltpu.VMEM((1, width), full),
            pltpu.VMEM((SIDE, rows, flat), low),
            pltpu.VMEM((SIDE, rows, flat), low),
            pltpu.VMEM((SIDE, rows, flat), low),
            pltpu.VMEM((SIDE, rows, flat), low),
            pltpu.VMEM((SIDE, rows, flat), low),
            pltpu.VMEM((SIDE, rows, flat), full),
            pltpu.VMEM((rows, flat), full),
            pltpu.VMEM((keys, flat), low),
            pltpu.VMEM((keys, flat), full),
            pltpu.VMEM((rows, flat), full),
            pltpu.VMEM((heads, width, keys), low),
            pltpu.VMEM((SIDE, heads, keys, rows), full),
            pltpu.VMEM((SIDE, heads, keys, rows), full),
            pltpu.VMEM((SIDE, 8, rows), full),
            pltpu.VMEM((SIDE, SIDE, 8, rows), full),
            pltpu.VMEM((keys, flat), full),
            pltpu.VMEM((keys, flat), full),
            pltpu.VMEM((SIDE, rows, flat), low),
            pltpu.VMEM((SIDE, rows, flat), low),
            pltpu.VMEM((SIDE, rows, flat), low),
            pltpu.VMEM((SIDE, rows, flat), low),
            pltpu.VMEM((rows, flat), low),
            pltpu.VMEM((rows, flat), low),
            pltpu.VMEM((SIDE, heads, rows, width), full),
            pltpu.VMEM((SIDE, heads, rows, width), low),
            pltpu.VMEM((SIDE, heads, rows, width), low),
            pltpu.VMEM((heads, rows, width), low),
            pltpu.VMEM((n_tp, 8, width), full),
            pltpu.VMEM((SIDE * n_dp, 8, width), full),
            pltpu.VMEM((SIDE, 8, width), full),
            pltpu.SemaphoreType.DMA((6,)),
            pltpu.SemaphoreType.DMA((copies,)),
            pltpu.SemaphoreType.DMA((copies,)),
        ],
        compiler_params=pltpu.CompilerParams(collective_id=0, has_side_effects=True),
    )(
        q_raw[0],
        k_raw[0],
        value[0],
        d_out[0],
        q_gain[None],
        k_gain[None],
    )
    return (dq[None], dk[None], dv[None], gains[0], gains[1])


def solution(mesh):
    split = P("dp", "ctx", "tp")
    return jax.shard_map(
        local,
        mesh=mesh,
        in_specs=(split, split, split, split, P(), P()),
        out_specs=(split, split, split, P(), P()),
        check_vma=False,
    )
```

```python
import functools

import jax
import jax.numpy as jnp
from jax import lax
from jax.experimental import pallas as pl
from jax.experimental.pallas import tpu as pltpu
from jax.sharding import PartitionSpec as P

EPSILON = 1e-06
SIDE = 4
MESH = pl.DeviceIdType.MESH


def kernel(
    sizes,
    q_hbm,
    k_hbm,
    v_hbm,
    o_hbm,
    q_gain_hbm,
    k_gain_hbm,
    grad_out,
    gain_out,
    q_gain_ref,
    k_gain_ref,
    q_raw,
    k_raw,
    v_all,
    o_all,
    q_normed,
    q_unit,
    q_inverse,
    k_normed,
    k_unit,
    k_inverse,
    k_turned,
    expo,
    dprob,
    stat_own,
    stat_in,
    dk_acc,
    dv_acc,
    dk_send,
    dv_send,
    dk_in,
    dv_in,
    dk_far,
    dv_far,
    dq_full,
    dq_send,
    dq_in,
    dq_far,
    gain_tp,
    gain_z,
    gain_x,
    load_sem,
    send_sem,
    recv_sem,
):
    n_tp, n_dp, heads, length = sizes
    rows = q_hbm.shape[0]
    width = q_gain_hbm.shape[1]
    keys = SIDE * rows
    scale = width ** (-0.5)
    ctx = lax.axis_index("ctx")
    tp = lax.axis_index("tp")
    dp = lax.axis_index("dp")
    x = lax.rem(ctx, SIDE)
    z = ctx // SIDE

    def along_x(step):
        return {"ctx": z * SIDE + lax.rem(x + step, SIDE), "tp": tp, "dp": dp}

    def along_z(step):
        return {"ctx": lax.rem(z + step, SIDE) * SIDE + x, "tp": tp, "dp": dp}

    def along_z_dp(step):
        place = lax.rem(z + step // n_dp, SIDE) * SIDE + x
        return {"ctx": place, "tp": tp, "dp": lax.rem(dp + step % n_dp, n_dp)}

    def along_tp(step):
        return {"ctx": ctx, "tp": lax.rem(tp + step, n_tp), "dp": dp}

    barrier = pltpu.get_barrier_semaphore()
    partners = (
        [along_z_dp(step) for step in range(1, SIDE * n_dp)]
        + [along_tp(step) for step in range(1, n_tp)]
        + [along_x(step) for step in range(1, SIDE)]
    )
    for partner in partners:
        pl.semaphore_signal(barrier, inc=1, device_id=partner, device_id_type=MESH)

    loads = [
        pltpu.make_async_copy(src, dst, load_sem.at[index])
        for index, (src, dst) in enumerate(
            (
                (q_gain_hbm, q_gain_ref),
                (k_gain_hbm, k_gain_ref),
                (k_hbm, k_raw.at[0]),
                (q_hbm, q_raw.at[0]),
                (v_hbm, v_all.at[0]),
                (o_hbm, o_all.at[0]),
            )
        )
    ]
    for one in loads:
        one.start()

    count = [0]
    started = []

    def copy(src, dst, device):
        index = count[0]
        count[0] += 1
        one = pltpu.make_async_remote_copy(
            src_ref=src,
            dst_ref=dst,
            send_sem=send_sem.at[index],
            recv_sem=recv_sem.at[index],
            device_id=device,
            device_id_type=MESH,
        )
        started.append(one)
        return one

    def cols(head):
        return slice(head * width, (head + 1) * width)

    pl.semaphore_wait(barrier, len(partners))

    q_up = copy(q_hbm, q_raw.at[1], along_z(1))
    q_down = copy(q_hbm, q_raw.at[3], along_z(3))
    o_up = copy(o_hbm, o_all.at[1], along_z(1))
    o_down = copy(o_hbm, o_all.at[3], along_z(3))
    k_up = copy(k_hbm, k_raw.at[1], along_x(1))
    k_down = copy(k_hbm, k_raw.at[3], along_x(3))
    v_up = copy(v_hbm, v_all.at[1], along_x(1))
    v_down = copy(v_hbm, v_all.at[3], along_x(3))
    for one in (q_up, o_down, k_up, v_down, o_up, q_down, v_up, k_down):
        one.start()
    q_far = copy(q_raw.at[1], q_raw.at[2], along_z(1))
    o_far = copy(o_all.at[3], o_all.at[2], along_z(3))
    k_far = copy(k_raw.at[1], k_raw.at[2], along_x(1))
    v_far = copy(v_all.at[3], v_all.at[2], along_x(3))

    dk_acc[...] = jnp.zeros_like(dk_acc)
    dv_acc[...] = jnp.zeros_like(dv_acc)
    stat_own[...] = jnp.zeros_like(stat_own)
    for one in loads:
        one.wait()

    def norm_q(slot):
        for head in range(heads):
            values = q_raw[slot, :, cols(head)].astype(jnp.float32)
            inverse = lax.rsqrt(jnp.mean(values * values, axis=1, keepdims=True) + EPSILON)
            unit = values * inverse
            q_unit[slot, :, cols(head)] = unit
            q_normed[slot, :, cols(head)] = (unit * q_gain_ref[...]).astype(jnp.bfloat16)
            if slot == 0:
                q_inverse[:, cols(head)] = jnp.broadcast_to(inverse, (rows, width))

    def norm_k(slot):
        here = slice(slot * rows, (slot + 1) * rows)
        for head in range(heads):
            values = k_raw[slot, :, cols(head)].astype(jnp.float32)
            inverse = lax.rsqrt(jnp.mean(values * values, axis=1, keepdims=True) + EPSILON)
            unit = values * inverse
            normed = (unit * k_gain_ref[...]).astype(jnp.bfloat16)
            k_unit[here, cols(head)] = unit
            k_normed[here, cols(head)] = normed
            k_turned[head, :, here] = normed.T
            if slot == 0:
                k_inverse[:, cols(head)] = jnp.broadcast_to(inverse, (rows, width))

    norm_q(0)
    norm_k(0)

    k_up.wait_recv()
    k_far.start()
    v_down.wait_recv()
    v_far.start()
    norm_k(1)
    k_down.wait_recv()
    norm_k(3)
    v_up.wait_recv()
    q_up.wait_recv()
    q_far.start()
    o_down.wait_recv()
    o_far.start()
    k_far.wait_recv()
    norm_k(2)
    v_far.wait_recv()

    def contract_last(left, right):
        return lax.dot_general(
            left, right, (((1,), (1,)), ((), ())), preferred_element_type=jnp.float32
        )

    stat_copies = {}

    def first_pass(slot):
        for head in range(heads):
            scores = (
                contract_last(k_normed[:, cols(head)], q_normed[slot, :, cols(head)]) * scale
            )
            top = jnp.max(scores, axis=0, keepdims=True)
            weights = jnp.exp(scores - top)
            slopes = contract_last(
                v_all[:, :, cols(head)].reshape(keys, width), o_all[slot, :, cols(head)]
            )
            expo[slot, head] = weights
            dprob[slot, head] = slopes
            stat_own[slot, 3 * head : 3 * head + 1] = top
            stat_own[slot, 3 * head + 1 : 3 * head + 2] = jnp.sum(weights, axis=0, keepdims=True)
            stat_own[slot, 3 * head + 2 : 3 * head + 3] = jnp.sum(
                weights * slopes, axis=0, keepdims=True
            )
        for step in (2, 1, 3):
            there = (slot + step) % SIDE
            one = copy(stat_own.at[slot], stat_in.at[there, step], along_z(step))
            stat_copies[there, step] = one
            one.start()

    first_pass(0)
    o_up.wait_recv()
    norm_q(1)
    first_pass(1)
    q_down.wait_recv()
    norm_q(3)
    first_pass(3)
    q_far.wait_recv()
    norm_q(2)
    o_far.wait_recv()
    first_pass(2)

    def second_pass(slot):
        for step in range(1, SIDE):
            stat_copies[slot, step].wait_recv()
        part = jnp.zeros((1, width), jnp.float32)
        for head in range(heads):
            tops = [stat_own[slot, 3 * head : 3 * head + 1]]
            totals = [stat_own[slot, 3 * head + 1 : 3 * head + 2]]
            weighted = [stat_own[slot, 3 * head + 2 : 3 * head + 3]]
            for step in range(1, SIDE):
                tops.append(stat_in[slot, step, 3 * head : 3 * head + 1])
                totals.append(stat_in[slot, step, 3 * head + 1 : 3 * head + 2])
                weighted.append(stat_in[slot, step, 3 * head + 2 : 3 * head + 3])
            top = functools.reduce(jnp.maximum, tops)
            factors = [jnp.exp(one - top) for one in tops]
            total = sum(one * factor for one, factor in zip(totals, factors))
            delta = sum(one * factor for one, factor in zip(weighted, factors)) / total
            prob = expo[slot, head] * (factors[0] / total)
            dscore = (prob * (dprob[slot, head] - delta) * scale).astype(jnp.bfloat16)
            prob_low = prob.astype(jnp.bfloat16)
            dq = jnp.dot(k_turned[head], dscore, preferred_element_type=jnp.float32).T
            part += jnp.sum(dq * q_unit[slot, :, cols(head)], axis=0, keepdims=True)
            dq_full[slot, head] = dq
            dk_acc[:, cols(head)] += jnp.dot(
                dscore, q_normed[slot, :, cols(head)], preferred_element_type=jnp.float32
            )
            dv_acc[:, cols(head)] += jnp.dot(
                prob_low, o_all[slot, :, cols(head)], preferred_element_type=jnp.float32
            )
        return part

    def via(head):
        return 1 if head % 2 == 0 else 3

    def start(src, dst, device):
        one = copy(src, dst, device)
        one.start()
        return one

    dq_far_copies, dq_copies = [], []
    q_gain_part = second_pass(2)
    for head in range(heads):
        dq_send[2, head] = dq_full[2, head].astype(jnp.bfloat16)
        device = along_z(SIDE - via(head))
        dq_far_copies.append(start(dq_send.at[2, head], dq_far.at[head], device))
    for slot in (1, 3):
        q_gain_part += second_pass(slot)
        for head in range(heads):
            if via(head) != slot:
                dq_send[slot, head] = dq_full[slot, head].astype(jnp.bfloat16)
                device = along_z(SIDE - slot)
                dq_copies.append(start(dq_send.at[slot, head], dq_in.at[slot, head], device))
    q_gain_part += second_pass(0)

    def block(slot):
        return slice(slot * rows, (slot + 1) * rows)

    dk_send[2] = dk_acc[block(2), :].astype(jnp.bfloat16)
    dk_far_copy = start(dk_send.at[2], dk_far, along_x(3))
    dv_send[2] = dv_acc[block(2), :].astype(jnp.bfloat16)
    dv_far_copy = start(dv_send.at[2], dv_far, along_x(1))
    dk_send[3] = dk_acc[block(3), :].astype(jnp.bfloat16)
    dk_near = start(dk_send.at[3], dk_in.at[3], along_x(1))
    dv_send[1] = dv_acc[block(1), :].astype(jnp.bfloat16)
    dv_near = start(dv_send.at[1], dv_in.at[1], along_x(3))

    k_gain_part = jnp.zeros((1, width), jnp.float32)
    for head in range(heads):
        k_gain_part += jnp.sum(
            dk_acc[:, cols(head)] * k_unit[:, cols(head)], axis=0, keepdims=True
        )
    part = jnp.concatenate([q_gain_part, k_gain_part], axis=0)

    def spread(buffer, size, place, device, part):
        buffer[place] = part
        return [
            start(buffer.at[place], buffer.at[place], device(step)) for step in range(1, size)
        ]

    def gathered(buffer, size, copies):
        for one in copies:
            one.wait_recv()
        part = buffer[0]
        for index in range(1, size):
            part += buffer[index]
        return part

    gain_copies = spread(gain_tp, n_tp, tp, along_tp, part)

    for head in range(heads):
        slot = via(head)
        dq_far_copies[head].wait_recv()
        total = dq_full[slot, head] + dq_far[head].astype(jnp.float32)
        dq_send[slot, head] = total.astype(jnp.bfloat16)
        device = along_z(SIDE - slot)
        dq_copies.append(start(dq_send.at[slot, head], dq_in.at[slot, head], device))

    part = gathered(gain_tp, n_tp, gain_copies)
    gain_copies = spread(gain_z, SIDE * n_dp, z * n_dp + dp, along_z_dp, part)

    dk_far_copy.wait_recv()
    total = dk_acc[block(1), :] + dk_far[...].astype(jnp.float32)
    dk_send[1] = total.astype(jnp.bfloat16)
    dk_last = start(dk_send.at[1], dk_in.at[1], along_x(3))
    dv_far_copy.wait_recv()
    total = dv_acc[block(3), :] + dv_far[...].astype(jnp.float32)
    dv_send[3] = total.astype(jnp.bfloat16)
    dv_last = start(dv_send.at[3], dv_in.at[3], along_x(1))

    def restore(grad, unit, inverse, gain):
        scaled = grad * gain
        return inverse * (scaled - unit * jnp.mean(scaled * unit, axis=1, keepdims=True))

    for one in dq_copies:
        one.wait_recv()
    for head in range(heads):
        grad = dq_full[0, head]
        for slot in (1, 3):
            grad += dq_in[slot, head].astype(jnp.float32)
        grad_out[0, :, cols(head)] = restore(
            grad, q_unit[0, :, cols(head)], q_inverse[:, cols(head)], q_gain_ref[...]
        ).astype(jnp.bfloat16)

    part = gathered(gain_z, SIDE * n_dp, gain_copies)
    gain_copies = spread(gain_x, SIDE, x, along_x, part)

    for one in (dk_near, dv_near, dk_last, dv_last):
        one.wait_recv()
    for head in range(heads):
        grad = dk_acc[block(0), cols(head)]
        total = dv_acc[block(0), cols(head)]
        for slot in (1, 3):
            grad += dk_in[slot, :, cols(head)].astype(jnp.float32)
            total += dv_in[slot, :, cols(head)].astype(jnp.float32)
        grad_out[1, :, cols(head)] = restore(
            grad, k_unit[block(0), cols(head)], k_inverse[:, cols(head)], k_gain_ref[...]
        ).astype(jnp.bfloat16)
        grad_out[2, :, cols(head)] = total.astype(jnp.bfloat16)

    gain_out[...] = gathered(gain_x, SIDE, gain_copies) / length
    for one in started:
        one.wait_send()


def local(q_raw, k_raw, value, d_out, q_gain, k_gain):
    width = q_gain.shape[0]
    rows, flat = q_raw.shape[1:]
    heads = flat // width
    n_ctx, n_tp, n_dp = (lax.axis_size(name) for name in ("ctx", "tp", "dp"))
    keys = SIDE * rows
    low, full = jnp.bfloat16, jnp.float32
    copies = 12 + 12 + 3 * heads + 6 + SIDE * n_dp - 1 + n_tp - 1 + SIDE - 1
    sizes = (n_tp, n_dp, heads, n_ctx * rows)
    block = jax.ShapeDtypeStruct((3, rows, flat), low)
    vmem = pl.BlockSpec(memory_space=pltpu.VMEM)
    grads, gains = pl.pallas_call(
        functools.partial(kernel, sizes),
        out_shape=(block, jax.ShapeDtypeStruct((2, width), full)),
        in_specs=[pl.BlockSpec(memory_space=pl.ANY)] * 6,
        out_specs=(vmem,) * 2,
        scratch_shapes=[
            pltpu.VMEM((1, width), full),
            pltpu.VMEM((1, width), full),
            pltpu.VMEM((SIDE, rows, flat), low),
            pltpu.VMEM((SIDE, rows, flat), low),
            pltpu.VMEM((SIDE, rows, flat), low),
            pltpu.VMEM((SIDE, rows, flat), low),
            pltpu.VMEM((SIDE, rows, flat), low),
            pltpu.VMEM((SIDE, rows, flat), full),
            pltpu.VMEM((rows, flat), full),
            pltpu.VMEM((keys, flat), low),
            pltpu.VMEM((keys, flat), full),
            pltpu.VMEM((rows, flat), full),
            pltpu.VMEM((heads, width, keys), low),
            pltpu.VMEM((SIDE, heads, keys, rows), full),
            pltpu.VMEM((SIDE, heads, keys, rows), full),
            pltpu.VMEM((SIDE, 8, rows), full),
            pltpu.VMEM((SIDE, SIDE, 8, rows), full),
            pltpu.VMEM((keys, flat), full),
            pltpu.VMEM((keys, flat), full),
            pltpu.VMEM((SIDE, rows, flat), low),
            pltpu.VMEM((SIDE, rows, flat), low),
            pltpu.VMEM((SIDE, rows, flat), low),
            pltpu.VMEM((SIDE, rows, flat), low),
            pltpu.VMEM((rows, flat), low),
            pltpu.VMEM((rows, flat), low),
            pltpu.VMEM((SIDE, heads, rows, width), full),
            pltpu.VMEM((SIDE, heads, rows, width), low),
            pltpu.VMEM((SIDE, heads, rows, width), low),
            pltpu.VMEM((heads, rows, width), low),
            pltpu.VMEM((n_tp, 2, width), full),
            pltpu.VMEM((SIDE * n_dp, 2, width), full),
            pltpu.VMEM((SIDE, 2, width), full),
            pltpu.SemaphoreType.DMA((6,)),
            pltpu.SemaphoreType.DMA((copies,)),
            pltpu.SemaphoreType.DMA((copies,)),
        ],
        compiler_params=pltpu.CompilerParams(collective_id=0, has_side_effects=True),
    )(
        q_raw[0],
        k_raw[0],
        value[0],
        d_out[0],
        q_gain[None],
        k_gain[None],
    )
    return (grads[0:1], grads[1:2], grads[2:3], gains[0], gains[1])


def solution(mesh):
    split = P("dp", "ctx", "tp")
    return jax.shard_map(
        local,
        mesh=mesh,
        in_specs=(split, split, split, split, P(), P()),
        out_specs=(split, split, split, P(), P()),
        check_vma=False,
    )
```

```python
import functools

import jax
import jax.numpy as jnp
from jax import lax
from jax.experimental import pallas as pl
from jax.experimental.pallas import tpu as pltpu
from jax.sharding import PartitionSpec as P

EPSILON = 1e-06
SIDE = 4
CORES = 2
MESH = pl.DeviceIdType.MESH


def kernel(
    sizes,
    q_hbm,
    k_hbm,
    v_hbm,
    o_hbm,
    q_gain_hbm,
    k_gain_hbm,
    grad_out,
    gain_out,
    q_gain_ref,
    k_gain_ref,
    q_raw,
    k_raw,
    v_all,
    o_all,
    q_normed,
    q_unit,
    q_inverse,
    k_normed,
    k_unit,
    k_inverse,
    k_turned,
    expo,
    dprob,
    stat_own,
    stat_in,
    dk_acc,
    dv_acc,
    dk_send,
    dv_send,
    dk_in,
    dv_in,
    dk_far,
    dv_far,
    dq_full,
    dq_send,
    dq_in,
    dq_far,
    gain_tp,
    gain_z,
    gain_x,
    load_sem,
    send_sem,
    recv_sem,
):
    n_tp, n_dp, heads, length = sizes
    rows = q_hbm.shape[0]
    width = q_gain_hbm.shape[1]
    keys = SIDE * rows
    scale = width ** (-0.5)
    ctx = lax.axis_index("ctx")
    tp = lax.axis_index("tp")
    dp = lax.axis_index("dp")
    x = lax.rem(ctx, SIDE)
    z = ctx // SIDE

    def along_x(step):
        return {"ctx": z * SIDE + lax.rem(x + step, SIDE), "tp": tp, "dp": dp}

    def along_z(step):
        return {"ctx": lax.rem(z + step, SIDE) * SIDE + x, "tp": tp, "dp": dp}

    chips = n_dp // CORES
    ring = SIDE * chips
    core = lax.rem(dp, CORES)
    z_place = z * chips + dp // CORES

    def along_ring(step):
        place = lax.rem(z_place + step, ring)
        return {
            "ctx": place // chips * SIDE + x,
            "tp": tp,
            "dp": lax.rem(place, chips) * CORES + core,
        }

    def along_x_core(step):
        return {
            "ctx": z * SIDE + lax.rem(x + step // CORES, SIDE),
            "tp": tp,
            "dp": dp - core + lax.rem(core + step % CORES, CORES),
        }

    def along_tp(step):
        return {"ctx": ctx, "tp": lax.rem(tp + step, n_tp), "dp": dp}

    barrier = pltpu.get_barrier_semaphore()

    def farthest_first(size):
        return sorted(range(1, size), key=lambda step: -min(step, size - step))

    partners = (
        [along_ring(step) for step in farthest_first(ring)]
        + [along_tp(step) for step in farthest_first(n_tp)]
        + [along_x_core(step) for step in farthest_first(SIDE * CORES)]
    )
    for partner in partners:
        pl.semaphore_signal(barrier, inc=1, device_id=partner, device_id_type=MESH)

    loads = [
        pltpu.make_async_copy(src, dst, load_sem.at[index])
        for index, (src, dst) in enumerate(
            (
                (q_gain_hbm, q_gain_ref),
                (k_gain_hbm, k_gain_ref),
                (k_hbm, k_raw.at[0]),
                (q_hbm, q_raw.at[0]),
                (v_hbm, v_all.at[0]),
                (o_hbm, o_all.at[0]),
            )
        )
    ]
    for one in loads:
        one.start()

    count = [0]
    started = []

    def copy(src, dst, device):
        index = count[0]
        count[0] += 1
        one = pltpu.make_async_remote_copy(
            src_ref=src,
            dst_ref=dst,
            send_sem=send_sem.at[index],
            recv_sem=recv_sem.at[index],
            device_id=device,
            device_id_type=MESH,
        )
        started.append(one)
        return one

    def cols(head):
        return slice(head * width, (head + 1) * width)

    pl.semaphore_wait(barrier, len(partners))

    q_up = copy(q_hbm, q_raw.at[1], along_z(1))
    q_down = copy(q_hbm, q_raw.at[3], along_z(3))
    o_up = copy(o_hbm, o_all.at[1], along_z(1))
    o_down = copy(o_hbm, o_all.at[3], along_z(3))
    k_up = copy(k_hbm, k_raw.at[1], along_x(1))
    k_down = copy(k_hbm, k_raw.at[3], along_x(3))
    v_up = copy(v_hbm, v_all.at[1], along_x(1))
    v_down = copy(v_hbm, v_all.at[3], along_x(3))
    for one in (q_up, o_down, k_up, v_down, o_up, q_down, v_up, k_down):
        one.start()
    q_far = copy(q_raw.at[1], q_raw.at[2], along_z(1))
    o_far = copy(o_all.at[3], o_all.at[2], along_z(3))
    k_far = copy(k_raw.at[1], k_raw.at[2], along_x(1))
    v_far = copy(v_all.at[3], v_all.at[2], along_x(3))

    dk_acc[...] = jnp.zeros_like(dk_acc)
    dv_acc[...] = jnp.zeros_like(dv_acc)
    stat_own[...] = jnp.zeros_like(stat_own)
    for one in loads:
        one.wait()

    def norm_q(slot):
        for head in range(heads):
            values = q_raw[slot, :, cols(head)].astype(jnp.float32)
            inverse = lax.rsqrt(jnp.mean(values * values, axis=1, keepdims=True) + EPSILON)
            unit = values * inverse
            q_unit[slot, :, cols(head)] = unit
            q_normed[slot, :, cols(head)] = (unit * q_gain_ref[...]).astype(jnp.bfloat16)
            if slot == 0:
                q_inverse[:, cols(head)] = jnp.broadcast_to(inverse, (rows, width))

    def norm_k(slot):
        here = slice(slot * rows, (slot + 1) * rows)
        for head in range(heads):
            values = k_raw[slot, :, cols(head)].astype(jnp.float32)
            inverse = lax.rsqrt(jnp.mean(values * values, axis=1, keepdims=True) + EPSILON)
            unit = values * inverse
            normed = (unit * k_gain_ref[...]).astype(jnp.bfloat16)
            k_unit[here, cols(head)] = unit
            k_normed[here, cols(head)] = normed
            k_turned[head, :, here] = normed.T
            if slot == 0:
                k_inverse[:, cols(head)] = jnp.broadcast_to(inverse, (rows, width))

    norm_q(0)
    norm_k(0)

    k_up.wait_recv()
    k_far.start()
    v_down.wait_recv()
    v_far.start()
    norm_k(1)
    k_down.wait_recv()
    norm_k(3)
    v_up.wait_recv()
    q_up.wait_recv()
    q_far.start()
    o_down.wait_recv()
    o_far.start()
    k_far.wait_recv()
    norm_k(2)
    v_far.wait_recv()

    def contract_last(left, right):
        return lax.dot_general(
            left, right, (((1,), (1,)), ((), ())), preferred_element_type=jnp.float32
        )

    stat_copies = {}

    def first_pass(slot):
        for head in range(heads):
            scores = (
                contract_last(k_normed[:, cols(head)], q_normed[slot, :, cols(head)]) * scale
            )
            top = jnp.max(scores, axis=0, keepdims=True)
            weights = jnp.exp(scores - top)
            slopes = contract_last(
                v_all[:, :, cols(head)].reshape(keys, width), o_all[slot, :, cols(head)]
            )
            expo[slot, head] = weights
            dprob[slot, head] = slopes
            stat_own[slot, 3 * head : 3 * head + 1] = top
            stat_own[slot, 3 * head + 1 : 3 * head + 2] = jnp.sum(weights, axis=0, keepdims=True)
            stat_own[slot, 3 * head + 2 : 3 * head + 3] = jnp.sum(
                weights * slopes, axis=0, keepdims=True
            )
        for step in (2, 1, 3):
            there = (slot + step) % SIDE
            one = copy(stat_own.at[slot], stat_in.at[there, step], along_z(step))
            stat_copies[there, step] = one
            one.start()

    first_pass(0)
    o_up.wait_recv()
    norm_q(1)
    first_pass(1)
    q_down.wait_recv()
    norm_q(3)
    first_pass(3)
    q_far.wait_recv()
    norm_q(2)
    o_far.wait_recv()
    first_pass(2)

    def second_pass(slot):
        for step in range(1, SIDE):
            stat_copies[slot, step].wait_recv()
        part = jnp.zeros((1, width), jnp.float32)
        for head in range(heads):
            tops = [stat_own[slot, 3 * head : 3 * head + 1]]
            totals = [stat_own[slot, 3 * head + 1 : 3 * head + 2]]
            weighted = [stat_own[slot, 3 * head + 2 : 3 * head + 3]]
            for step in range(1, SIDE):
                tops.append(stat_in[slot, step, 3 * head : 3 * head + 1])
                totals.append(stat_in[slot, step, 3 * head + 1 : 3 * head + 2])
                weighted.append(stat_in[slot, step, 3 * head + 2 : 3 * head + 3])
            top = functools.reduce(jnp.maximum, tops)
            factors = [jnp.exp(one - top) for one in tops]
            total = sum(one * factor for one, factor in zip(totals, factors))
            delta = sum(one * factor for one, factor in zip(weighted, factors)) / total
            prob = expo[slot, head] * (factors[0] / total)
            dscore = (prob * (dprob[slot, head] - delta) * scale).astype(jnp.bfloat16)
            prob_low = prob.astype(jnp.bfloat16)
            dq = jnp.dot(k_turned[head], dscore, preferred_element_type=jnp.float32).T
            part += jnp.sum(dq * q_unit[slot, :, cols(head)], axis=0, keepdims=True)
            dq_full[slot, head] = dq
            dk_acc[:, cols(head)] += jnp.dot(
                dscore, q_normed[slot, :, cols(head)], preferred_element_type=jnp.float32
            )
            dv_acc[:, cols(head)] += jnp.dot(
                prob_low, o_all[slot, :, cols(head)], preferred_element_type=jnp.float32
            )
        return part

    def via(head):
        return 1 if head % 2 == 0 else 3

    def start(src, dst, device):
        one = copy(src, dst, device)
        one.start()
        return one

    dq_far_copies, dq_copies = [], []
    q_gain_part = second_pass(2)
    for head in range(heads):
        dq_send[2, head] = dq_full[2, head].astype(jnp.bfloat16)
        device = along_z(SIDE - via(head))
        dq_far_copies.append(start(dq_send.at[2, head], dq_far.at[head], device))
    for slot in (1, 3):
        q_gain_part += second_pass(slot)
        for head in range(heads):
            if via(head) != slot:
                dq_send[slot, head] = dq_full[slot, head].astype(jnp.bfloat16)
                device = along_z(SIDE - slot)
                dq_copies.append(start(dq_send.at[slot, head], dq_in.at[slot, head], device))
    q_gain_part += second_pass(0)

    def block(slot):
        return slice(slot * rows, (slot + 1) * rows)

    k_gain_part = jnp.zeros((1, width), jnp.float32)
    for head in range(heads):
        k_gain_part += jnp.sum(
            dk_acc[:, cols(head)] * k_unit[:, cols(head)], axis=0, keepdims=True
        )
    part = jnp.concatenate([q_gain_part, k_gain_part], axis=0)

    def spread(buffer, size, place, device, part):
        buffer[place] = part
        return [
            start(buffer.at[place], buffer.at[place], device(step))
            for step in farthest_first(size)
        ]

    def gathered(buffer, size, copies):
        for one in copies:
            one.wait_recv()
        part = buffer[0]
        for index in range(1, size):
            part += buffer[index]
        return part

    gain_copies = spread(gain_tp, n_tp, tp, along_tp, part)

    dk_send[2] = dk_acc[block(2), :].astype(jnp.bfloat16)
    dk_far_copy = start(dk_send.at[2], dk_far, along_x(3))
    dv_send[2] = dv_acc[block(2), :].astype(jnp.bfloat16)
    dv_far_copy = start(dv_send.at[2], dv_far, along_x(1))
    dk_send[3] = dk_acc[block(3), :].astype(jnp.bfloat16)
    dk_near = start(dk_send.at[3], dk_in.at[3], along_x(1))
    dv_send[1] = dv_acc[block(1), :].astype(jnp.bfloat16)
    dv_near = start(dv_send.at[1], dv_in.at[1], along_x(3))

    for head in range(heads):
        slot = via(head)
        dq_far_copies[head].wait_recv()
        total = dq_full[slot, head] + dq_far[head].astype(jnp.float32)
        dq_send[slot, head] = total.astype(jnp.bfloat16)
        device = along_z(SIDE - slot)
        dq_copies.append(start(dq_send.at[slot, head], dq_in.at[slot, head], device))

    part = gathered(gain_tp, n_tp, gain_copies)
    gain_copies = spread(gain_z, ring, z_place, along_ring, part)

    dk_far_copy.wait_recv()
    total = dk_acc[block(1), :] + dk_far[...].astype(jnp.float32)
    dk_send[1] = total.astype(jnp.bfloat16)
    dk_last = start(dk_send.at[1], dk_in.at[1], along_x(3))
    dv_far_copy.wait_recv()
    total = dv_acc[block(3), :] + dv_far[...].astype(jnp.float32)
    dv_send[3] = total.astype(jnp.bfloat16)
    dv_last = start(dv_send.at[3], dv_in.at[3], along_x(1))

    def restore(grad, unit, inverse, gain):
        scaled = grad * gain
        return inverse * (scaled - unit * jnp.mean(scaled * unit, axis=1, keepdims=True))

    for one in dq_copies:
        one.wait_recv()
    for head in range(heads):
        grad = dq_full[0, head]
        for slot in (1, 3):
            grad += dq_in[slot, head].astype(jnp.float32)
        grad_out[0, :, cols(head)] = restore(
            grad, q_unit[0, :, cols(head)], q_inverse[:, cols(head)], q_gain_ref[...]
        ).astype(jnp.bfloat16)

    part = gathered(gain_z, ring, gain_copies)
    gain_copies = spread(gain_x, SIDE * CORES, x * CORES + core, along_x_core, part)

    for one in (dk_near, dv_near, dk_last, dv_last):
        one.wait_recv()
    for head in range(heads):
        grad = dk_acc[block(0), cols(head)]
        total = dv_acc[block(0), cols(head)]
        for slot in (1, 3):
            grad += dk_in[slot, :, cols(head)].astype(jnp.float32)
            total += dv_in[slot, :, cols(head)].astype(jnp.float32)
        grad_out[1, :, cols(head)] = restore(
            grad, k_unit[block(0), cols(head)], k_inverse[:, cols(head)], k_gain_ref[...]
        ).astype(jnp.bfloat16)
        grad_out[2, :, cols(head)] = total.astype(jnp.bfloat16)

    gain_out[...] = gathered(gain_x, SIDE * CORES, gain_copies) / length
    for one in started:
        one.wait_send()


def deliver(grad_in, gain_in, dq_out, dk_out, dv_out, q_gain_out, k_gain_out, sem):
    pairs = (
        (grad_in.at[0], dq_out.at[0]),
        (grad_in.at[1], dk_out.at[0]),
        (grad_in.at[2], dv_out.at[0]),
    )
    copies = [pltpu.make_async_copy(a, b, sem.at[i]) for i, (a, b) in enumerate(pairs)]
    for one in copies:
        one.start()
    q_gain_out[...] = gain_in[0:1]
    k_gain_out[...] = gain_in[1:2]
    for one in copies:
        one.wait()


def local(q_raw, k_raw, value, d_out, q_gain, k_gain):
    width = q_gain.shape[0]
    rows, flat = q_raw.shape[1:]
    heads = flat // width
    n_ctx, n_tp, n_dp = (lax.axis_size(name) for name in ("ctx", "tp", "dp"))
    keys = SIDE * rows
    low, full = jnp.bfloat16, jnp.float32
    copies = 12 + 12 + 3 * heads + 6 + SIDE * n_dp // CORES - 1 + n_tp - 1 + SIDE * CORES - 1
    sizes = (n_tp, n_dp, heads, n_ctx * rows)
    block = jax.ShapeDtypeStruct((3, rows, flat), low)
    vmem = pl.BlockSpec(memory_space=pltpu.VMEM)
    grads, gains = pl.pallas_call(
        functools.partial(kernel, sizes),
        out_shape=(block, jax.ShapeDtypeStruct((2, width), full)),
        in_specs=[pl.BlockSpec(memory_space=pl.ANY)] * 6,
        out_specs=(vmem,) * 2,
        scratch_shapes=[
            pltpu.VMEM((1, width), full),
            pltpu.VMEM((1, width), full),
            pltpu.VMEM((SIDE, rows, flat), low),
            pltpu.VMEM((SIDE, rows, flat), low),
            pltpu.VMEM((SIDE, rows, flat), low),
            pltpu.VMEM((SIDE, rows, flat), low),
            pltpu.VMEM((SIDE, rows, flat), low),
            pltpu.VMEM((SIDE, rows, flat), full),
            pltpu.VMEM((rows, flat), full),
            pltpu.VMEM((keys, flat), low),
            pltpu.VMEM((keys, flat), full),
            pltpu.VMEM((rows, flat), full),
            pltpu.VMEM((heads, width, keys), low),
            pltpu.VMEM((SIDE, heads, keys, rows), full),
            pltpu.VMEM((SIDE, heads, keys, rows), full),
            pltpu.VMEM((SIDE, 8, rows), full),
            pltpu.VMEM((SIDE, SIDE, 8, rows), full),
            pltpu.VMEM((keys, flat), full),
            pltpu.VMEM((keys, flat), full),
            pltpu.VMEM((SIDE, rows, flat), low),
            pltpu.VMEM((SIDE, rows, flat), low),
            pltpu.VMEM((SIDE, rows, flat), low),
            pltpu.VMEM((SIDE, rows, flat), low),
            pltpu.VMEM((rows, flat), low),
            pltpu.VMEM((rows, flat), low),
            pltpu.VMEM((SIDE, heads, rows, width), full),
            pltpu.VMEM((SIDE, heads, rows, width), low),
            pltpu.VMEM((SIDE, heads, rows, width), low),
            pltpu.VMEM((heads, rows, width), low),
            pltpu.VMEM((n_tp, 2, width), full),
            pltpu.VMEM((SIDE * n_dp // CORES, 2, width), full),
            pltpu.VMEM((SIDE * CORES, 2, width), full),
            pltpu.SemaphoreType.DMA((6,)),
            pltpu.SemaphoreType.DMA((copies,)),
            pltpu.SemaphoreType.DMA((copies,)),
        ],
        compiler_params=pltpu.CompilerParams(collective_id=0, has_side_effects=True),
    )(
        q_raw[0],
        k_raw[0],
        value[0],
        d_out[0],
        q_gain[None],
        k_gain[None],
    )
    one = jax.ShapeDtypeStruct((1, rows, flat), low)
    line = jax.ShapeDtypeStruct((1, width), full)
    hbm = pl.BlockSpec(memory_space=pl.ANY)
    dq, dk, dv, q_part, k_part = pl.pallas_call(
        deliver,
        out_shape=(one, one, one, line, line),
        in_specs=[vmem, vmem],
        out_specs=(hbm, hbm, hbm, vmem, vmem),
        scratch_shapes=[pltpu.SemaphoreType.DMA((3,))],
    )(grads, gains)
    return (dq, dk, dv, q_part[0], k_part[0])


def solution(mesh):
    split = P("dp", "ctx", "tp")
    return jax.shard_map(
        local,
        mesh=mesh,
        in_specs=(split, split, split, split, P(), P()),
        out_specs=(split, split, split, P(), P()),
        check_vma=False,
    )
```

```python
import functools

import jax
import jax.numpy as jnp
from jax import lax
from jax.experimental import pallas as pl
from jax.experimental.pallas import tpu as pltpu
from jax.sharding import PartitionSpec as P

EPSILON = 1e-06
SIDE = 4
CORES = 2
MESH = pl.DeviceIdType.MESH


def kernel(
    sizes,
    q_hbm,
    k_hbm,
    v_hbm,
    o_hbm,
    q_gain_hbm,
    k_gain_hbm,
    grad_out,
    gain_out,
    q_gain_ref,
    k_gain_ref,
    q_raw,
    k_raw,
    v_all,
    o_all,
    q_normed,
    q_unit,
    q_inverse,
    k_normed,
    k_unit,
    k_inverse,
    k_turned,
    expo,
    dprob,
    stat_own,
    stat_in,
    dk_acc,
    dv_acc,
    dk_send,
    dv_send,
    dk_in,
    dv_in,
    dk_far,
    dv_far,
    dq_full,
    dq_send,
    dq_in,
    dq_far,
    gain_tp,
    gain_z,
    load_sem,
    send_sem,
    recv_sem,
):
    n_tp, n_dp, heads, length = sizes
    rows = q_hbm.shape[0]
    width = q_gain_hbm.shape[1]
    keys = SIDE * rows
    scale = width ** (-0.5)
    ctx = lax.axis_index("ctx")
    tp = lax.axis_index("tp")
    dp = lax.axis_index("dp")
    x = lax.rem(ctx, SIDE)
    z = ctx // SIDE

    def along_x(step):
        return {"ctx": z * SIDE + lax.rem(x + step, SIDE), "tp": tp, "dp": dp}

    def along_z(step):
        return {"ctx": lax.rem(z + step, SIDE) * SIDE + x, "tp": tp, "dp": dp}

    chips = n_dp // CORES
    ring = SIDE * chips
    core = lax.rem(dp, CORES)
    z_place = z * chips + dp // CORES

    def along_ring_x(step):
        place = lax.rem(z_place + step // SIDE, ring)
        return {
            "ctx": place // chips * SIDE + lax.rem(x + step % SIDE, SIDE),
            "tp": tp,
            "dp": lax.rem(place, chips) * CORES + core,
        }

    def along_tp_core(step):
        return {
            "ctx": ctx,
            "tp": lax.rem(tp + step // CORES, n_tp),
            "dp": dp - core + lax.rem(core + step % CORES, CORES),
        }

    def farthest_first(outer, inner):
        def hops(step):
            far, near = step // inner, step % inner
            return min(far, outer - far) + min(near, inner - near)

        return sorted(range(1, outer * inner), key=lambda step: -hops(step))

    ring_steps = farthest_first(ring, SIDE)
    tp_steps = farthest_first(n_tp, CORES)

    barrier = pltpu.get_barrier_semaphore()
    partners = [along_ring_x(step) for step in ring_steps] + [
        along_tp_core(step) for step in tp_steps
    ]
    for partner in partners:
        pl.semaphore_signal(barrier, inc=1, device_id=partner, device_id_type=MESH)

    loads = [
        pltpu.make_async_copy(src, dst, load_sem.at[index])
        for index, (src, dst) in enumerate(
            (
                (q_gain_hbm, q_gain_ref),
                (k_gain_hbm, k_gain_ref),
                (k_hbm, k_raw.at[0]),
                (q_hbm, q_raw.at[0]),
                (v_hbm, v_all.at[0]),
                (o_hbm, o_all.at[0]),
            )
        )
    ]
    for one in loads:
        one.start()

    count = [0]
    started = []

    def copy(src, dst, device):
        index = count[0]
        count[0] += 1
        one = pltpu.make_async_remote_copy(
            src_ref=src,
            dst_ref=dst,
            send_sem=send_sem.at[index],
            recv_sem=recv_sem.at[index],
            device_id=device,
            device_id_type=MESH,
        )
        started.append(one)
        return one

    def cols(head):
        return slice(head * width, (head + 1) * width)

    pl.semaphore_wait(barrier, len(partners))

    q_up = copy(q_hbm, q_raw.at[1], along_z(1))
    q_down = copy(q_hbm, q_raw.at[3], along_z(3))
    o_up = copy(o_hbm, o_all.at[1], along_z(1))
    o_down = copy(o_hbm, o_all.at[3], along_z(3))
    k_up = copy(k_hbm, k_raw.at[1], along_x(1))
    k_down = copy(k_hbm, k_raw.at[3], along_x(3))
    v_up = copy(v_hbm, v_all.at[1], along_x(1))
    v_down = copy(v_hbm, v_all.at[3], along_x(3))
    for one in (q_up, o_down, k_up, v_down, o_up, q_down, v_up, k_down):
        one.start()
    q_far = copy(q_raw.at[1], q_raw.at[2], along_z(1))
    o_far = copy(o_all.at[3], o_all.at[2], along_z(3))
    k_far = copy(k_raw.at[1], k_raw.at[2], along_x(1))
    v_far = copy(v_all.at[3], v_all.at[2], along_x(3))

    dk_acc[...] = jnp.zeros_like(dk_acc)
    dv_acc[...] = jnp.zeros_like(dv_acc)
    stat_own[...] = jnp.zeros_like(stat_own)
    for one in loads:
        one.wait()

    def norm_q(slot):
        for head in range(heads):
            values = q_raw[slot, :, cols(head)].astype(jnp.float32)
            inverse = lax.rsqrt(jnp.mean(values * values, axis=1, keepdims=True) + EPSILON)
            unit = values * inverse
            q_unit[slot, :, cols(head)] = unit
            q_normed[slot, :, cols(head)] = (unit * q_gain_ref[...]).astype(jnp.bfloat16)
            if slot == 0:
                q_inverse[:, cols(head)] = jnp.broadcast_to(inverse, (rows, width))

    def norm_k(slot):
        here = slice(slot * rows, (slot + 1) * rows)
        for head in range(heads):
            values = k_raw[slot, :, cols(head)].astype(jnp.float32)
            inverse = lax.rsqrt(jnp.mean(values * values, axis=1, keepdims=True) + EPSILON)
            unit = values * inverse
            normed = (unit * k_gain_ref[...]).astype(jnp.bfloat16)
            k_unit[here, cols(head)] = unit
            k_normed[here, cols(head)] = normed
            k_turned[head, :, here] = normed.T
            if slot == 0:
                k_inverse[:, cols(head)] = jnp.broadcast_to(inverse, (rows, width))

    norm_q(0)
    norm_k(0)

    k_up.wait_recv()
    k_far.start()
    v_down.wait_recv()
    v_far.start()
    norm_k(1)
    k_down.wait_recv()
    norm_k(3)
    v_up.wait_recv()
    q_up.wait_recv()
    q_far.start()
    o_down.wait_recv()
    o_far.start()
    k_far.wait_recv()
    norm_k(2)
    v_far.wait_recv()

    def contract_last(left, right):
        return lax.dot_general(
            left, right, (((1,), (1,)), ((), ())), preferred_element_type=jnp.float32
        )

    stat_copies = {}

    def first_pass(slot):
        for head in range(heads):
            scores = (
                contract_last(k_normed[:, cols(head)], q_normed[slot, :, cols(head)]) * scale
            )
            top = jnp.max(scores, axis=0, keepdims=True)
            weights = jnp.exp(scores - top)
            slopes = contract_last(
                v_all[:, :, cols(head)].reshape(keys, width), o_all[slot, :, cols(head)]
            )
            expo[slot, head] = weights
            dprob[slot, head] = slopes
            stat_own[slot, 3 * head : 3 * head + 1] = top
            stat_own[slot, 3 * head + 1 : 3 * head + 2] = jnp.sum(weights, axis=0, keepdims=True)
            stat_own[slot, 3 * head + 2 : 3 * head + 3] = jnp.sum(
                weights * slopes, axis=0, keepdims=True
            )
        for step in (2, 1, 3):
            there = (slot + step) % SIDE
            one = copy(stat_own.at[slot], stat_in.at[there, step], along_z(step))
            stat_copies[there, step] = one
            one.start()

    first_pass(0)
    o_up.wait_recv()
    norm_q(1)
    first_pass(1)
    q_down.wait_recv()
    norm_q(3)
    first_pass(3)
    q_far.wait_recv()
    norm_q(2)
    o_far.wait_recv()
    first_pass(2)

    def second_pass(slot):
        for step in range(1, SIDE):
            stat_copies[slot, step].wait_recv()
        part = jnp.zeros((1, width), jnp.float32)
        for head in range(heads):
            tops = [stat_own[slot, 3 * head : 3 * head + 1]]
            totals = [stat_own[slot, 3 * head + 1 : 3 * head + 2]]
            weighted = [stat_own[slot, 3 * head + 2 : 3 * head + 3]]
            for step in range(1, SIDE):
                tops.append(stat_in[slot, step, 3 * head : 3 * head + 1])
                totals.append(stat_in[slot, step, 3 * head + 1 : 3 * head + 2])
                weighted.append(stat_in[slot, step, 3 * head + 2 : 3 * head + 3])
            top = functools.reduce(jnp.maximum, tops)
            factors = [jnp.exp(one - top) for one in tops]
            total = sum(one * factor for one, factor in zip(totals, factors))
            delta = sum(one * factor for one, factor in zip(weighted, factors)) / total
            prob = expo[slot, head] * (factors[0] / total)
            dscore = (prob * (dprob[slot, head] - delta) * scale).astype(jnp.bfloat16)
            prob_low = prob.astype(jnp.bfloat16)
            dq = jnp.dot(k_turned[head], dscore, preferred_element_type=jnp.float32).T
            part += jnp.sum(dq * q_unit[slot, :, cols(head)], axis=0, keepdims=True)
            dq_full[slot, head] = dq
            dk_acc[:, cols(head)] += jnp.dot(
                dscore, q_normed[slot, :, cols(head)], preferred_element_type=jnp.float32
            )
            dv_acc[:, cols(head)] += jnp.dot(
                prob_low, o_all[slot, :, cols(head)], preferred_element_type=jnp.float32
            )
        return part

    def via(head):
        return 1 if head % 2 == 0 else 3

    def start(src, dst, device):
        one = copy(src, dst, device)
        one.start()
        return one

    dq_far_copies, dq_copies = [], []
    q_gain_part = second_pass(2)
    for head in range(heads):
        dq_send[2, head] = dq_full[2, head].astype(jnp.bfloat16)
        device = along_z(SIDE - via(head))
        dq_far_copies.append(start(dq_send.at[2, head], dq_far.at[head], device))
    for slot in (1, 3):
        q_gain_part += second_pass(slot)
        for head in range(heads):
            if via(head) != slot:
                dq_send[slot, head] = dq_full[slot, head].astype(jnp.bfloat16)
                device = along_z(SIDE - slot)
                dq_copies.append(start(dq_send.at[slot, head], dq_in.at[slot, head], device))
    q_gain_part += second_pass(0)

    def block(slot):
        return slice(slot * rows, (slot + 1) * rows)

    k_gain_part = jnp.zeros((1, width), jnp.float32)
    for head in range(heads):
        k_gain_part += jnp.sum(
            dk_acc[:, cols(head)] * k_unit[:, cols(head)], axis=0, keepdims=True
        )
    part = jnp.concatenate([q_gain_part, k_gain_part], axis=0)

    def spread(buffer, steps, place, device, part):
        buffer[place] = part
        return [start(buffer.at[place], buffer.at[place], device(step)) for step in steps]

    def gathered(buffer, copies):
        for one in copies:
            one.wait_recv()
        part = buffer[0]
        for index in range(1, len(copies) + 1):
            part += buffer[index]
        return part

    gain_copies = spread(gain_tp, tp_steps, tp * CORES + core, along_tp_core, part)

    dk_send[2] = dk_acc[block(2), :].astype(jnp.bfloat16)
    dk_far_copy = start(dk_send.at[2], dk_far, along_x(3))
    dv_send[2] = dv_acc[block(2), :].astype(jnp.bfloat16)
    dv_far_copy = start(dv_send.at[2], dv_far, along_x(1))
    dk_send[3] = dk_acc[block(3), :].astype(jnp.bfloat16)
    dk_near = start(dk_send.at[3], dk_in.at[3], along_x(1))
    dv_send[1] = dv_acc[block(1), :].astype(jnp.bfloat16)
    dv_near = start(dv_send.at[1], dv_in.at[1], along_x(3))

    for head in range(heads):
        slot = via(head)
        dq_far_copies[head].wait_recv()
        total = dq_full[slot, head] + dq_far[head].astype(jnp.float32)
        dq_send[slot, head] = total.astype(jnp.bfloat16)
        device = along_z(SIDE - slot)
        dq_copies.append(start(dq_send.at[slot, head], dq_in.at[slot, head], device))

    dk_far_copy.wait_recv()
    total = dk_acc[block(1), :] + dk_far[...].astype(jnp.float32)
    dk_send[1] = total.astype(jnp.bfloat16)
    dk_last = start(dk_send.at[1], dk_in.at[1], along_x(3))
    dv_far_copy.wait_recv()
    total = dv_acc[block(3), :] + dv_far[...].astype(jnp.float32)
    dv_send[3] = total.astype(jnp.bfloat16)
    dv_last = start(dv_send.at[3], dv_in.at[3], along_x(1))

    part = gathered(gain_tp, gain_copies)
    gain_copies = spread(gain_z, ring_steps, z_place * SIDE + x, along_ring_x, part)

    def restore(grad, unit, inverse, gain):
        scaled = grad * gain
        return inverse * (scaled - unit * jnp.mean(scaled * unit, axis=1, keepdims=True))

    for one in dq_copies:
        one.wait_recv()
    for head in range(heads):
        grad = dq_full[0, head]
        for slot in (1, 3):
            grad += dq_in[slot, head].astype(jnp.float32)
        grad_out[0, :, cols(head)] = restore(
            grad, q_unit[0, :, cols(head)], q_inverse[:, cols(head)], q_gain_ref[...]
        ).astype(jnp.bfloat16)

    for one in (dk_near, dv_near, dk_last, dv_last):
        one.wait_recv()
    for head in range(heads):
        grad = dk_acc[block(0), cols(head)]
        total = dv_acc[block(0), cols(head)]
        for slot in (1, 3):
            grad += dk_in[slot, :, cols(head)].astype(jnp.float32)
            total += dv_in[slot, :, cols(head)].astype(jnp.float32)
        grad_out[1, :, cols(head)] = restore(
            grad, k_unit[block(0), cols(head)], k_inverse[:, cols(head)], k_gain_ref[...]
        ).astype(jnp.bfloat16)
        grad_out[2, :, cols(head)] = total.astype(jnp.bfloat16)

    gain_out[...] = gathered(gain_z, gain_copies) / length
    for one in started:
        one.wait_send()


def deliver(grad_in, gain_in, dq_out, dk_out, dv_out, q_gain_out, k_gain_out, sem):
    pairs = (
        (grad_in.at[0], dq_out.at[0]),
        (grad_in.at[1], dk_out.at[0]),
        (grad_in.at[2], dv_out.at[0]),
    )
    copies = [pltpu.make_async_copy(a, b, sem.at[i]) for i, (a, b) in enumerate(pairs)]
    for one in copies:
        one.start()
    q_gain_out[...] = gain_in[0:1]
    k_gain_out[...] = gain_in[1:2]
    for one in copies:
        one.wait()


def local(q_raw, k_raw, value, d_out, q_gain, k_gain):
    width = q_gain.shape[0]
    rows, flat = q_raw.shape[1:]
    heads = flat // width
    n_ctx, n_tp, n_dp = (lax.axis_size(name) for name in ("ctx", "tp", "dp"))
    keys = SIDE * rows
    low, full = jnp.bfloat16, jnp.float32
    copies = 12 + 12 + 3 * heads + 6 + SIDE * SIDE * n_dp // CORES - 1 + n_tp * CORES - 1
    sizes = (n_tp, n_dp, heads, n_ctx * rows)
    block = jax.ShapeDtypeStruct((3, rows, flat), low)
    vmem = pl.BlockSpec(memory_space=pltpu.VMEM)
    grads, gains = pl.pallas_call(
        functools.partial(kernel, sizes),
        out_shape=(block, jax.ShapeDtypeStruct((2, width), full)),
        in_specs=[pl.BlockSpec(memory_space=pl.ANY)] * 6,
        out_specs=(vmem,) * 2,
        scratch_shapes=[
            pltpu.VMEM((1, width), full),
            pltpu.VMEM((1, width), full),
            pltpu.VMEM((SIDE, rows, flat), low),
            pltpu.VMEM((SIDE, rows, flat), low),
            pltpu.VMEM((SIDE, rows, flat), low),
            pltpu.VMEM((SIDE, rows, flat), low),
            pltpu.VMEM((SIDE, rows, flat), low),
            pltpu.VMEM((SIDE, rows, flat), full),
            pltpu.VMEM((rows, flat), full),
            pltpu.VMEM((keys, flat), low),
            pltpu.VMEM((keys, flat), full),
            pltpu.VMEM((rows, flat), full),
            pltpu.VMEM((heads, width, keys), low),
            pltpu.VMEM((SIDE, heads, keys, rows), full),
            pltpu.VMEM((SIDE, heads, keys, rows), full),
            pltpu.VMEM((SIDE, 8, rows), full),
            pltpu.VMEM((SIDE, SIDE, 8, rows), full),
            pltpu.VMEM((keys, flat), full),
            pltpu.VMEM((keys, flat), full),
            pltpu.VMEM((SIDE, rows, flat), low),
            pltpu.VMEM((SIDE, rows, flat), low),
            pltpu.VMEM((SIDE, rows, flat), low),
            pltpu.VMEM((SIDE, rows, flat), low),
            pltpu.VMEM((rows, flat), low),
            pltpu.VMEM((rows, flat), low),
            pltpu.VMEM((SIDE, heads, rows, width), full),
            pltpu.VMEM((SIDE, heads, rows, width), low),
            pltpu.VMEM((SIDE, heads, rows, width), low),
            pltpu.VMEM((heads, rows, width), low),
            pltpu.VMEM((n_tp * CORES, 2, width), full),
            pltpu.VMEM((SIDE * SIDE * n_dp // CORES, 2, width), full),
            pltpu.SemaphoreType.DMA((6,)),
            pltpu.SemaphoreType.DMA((copies,)),
            pltpu.SemaphoreType.DMA((copies,)),
        ],
        compiler_params=pltpu.CompilerParams(collective_id=0, has_side_effects=True),
    )(
        q_raw[0],
        k_raw[0],
        value[0],
        d_out[0],
        q_gain[None],
        k_gain[None],
    )
    one = jax.ShapeDtypeStruct((1, rows, flat), low)
    line = jax.ShapeDtypeStruct((1, width), full)
    hbm = pl.BlockSpec(memory_space=pl.ANY)
    dq, dk, dv, q_part, k_part = pl.pallas_call(
        deliver,
        out_shape=(one, one, one, line, line),
        in_specs=[vmem, vmem],
        out_specs=(hbm, hbm, hbm, vmem, vmem),
        scratch_shapes=[pltpu.SemaphoreType.DMA((3,))],
    )(grads, gains)
    return (dq, dk, dv, q_part[0], k_part[0])


def solution(mesh):
    split = P("dp", "ctx", "tp")
    return jax.shard_map(
        local,
        mesh=mesh,
        in_specs=(split, split, split, split, P(), P()),
        out_specs=(split, split, split, P(), P()),
        check_vma=False,
    )
```

```python
import functools

import jax
import jax.numpy as jnp
from jax import lax
from jax.experimental import pallas as pl
from jax.experimental.pallas import tpu as pltpu
from jax.sharding import PartitionSpec as P

EPSILON = 1e-06
SIDE = 4
CORES = 2
MESH = pl.DeviceIdType.MESH


def kernel(
    sizes,
    q_hbm,
    k_hbm,
    v_hbm,
    o_hbm,
    q_gain_hbm,
    k_gain_hbm,
    grad_out,
    gain_out,
    q_gain_ref,
    k_gain_ref,
    q_raw,
    k_raw,
    v_all,
    o_all,
    q_normed,
    q_unit,
    q_inverse,
    k_normed,
    k_unit,
    k_inverse,
    k_turned,
    expo,
    dprob,
    stat_own,
    stat_in,
    dk_acc,
    dv_acc,
    dk_send,
    dv_send,
    dk_in,
    dv_in,
    dk_far,
    dv_far,
    dq_full,
    dq_send,
    dq_in,
    dq_far,
    gain_tp,
    gain_z,
    load_sem,
    send_sem,
    recv_sem,
):
    n_tp, n_dp, heads, length = sizes
    rows = q_hbm.shape[0]
    width = q_gain_hbm.shape[1]
    keys = SIDE * rows
    scale = width ** (-0.5)
    ctx = lax.axis_index("ctx")
    tp = lax.axis_index("tp")
    dp = lax.axis_index("dp")
    x = lax.rem(ctx, SIDE)
    z = ctx // SIDE

    def along_x(step):
        return {"ctx": z * SIDE + lax.rem(x + step, SIDE), "tp": tp, "dp": dp}

    def along_z(step):
        return {"ctx": lax.rem(z + step, SIDE) * SIDE + x, "tp": tp, "dp": dp}

    chips = n_dp // CORES
    ring = SIDE * chips
    core = lax.rem(dp, CORES)
    z_place = z * chips + dp // CORES

    def along_ring_x(step):
        place = lax.rem(z_place + step // SIDE, ring)
        return {
            "ctx": place // chips * SIDE + lax.rem(x + step % SIDE, SIDE),
            "tp": tp,
            "dp": lax.rem(place, chips) * CORES + core,
        }

    def along_tp_core(step):
        return {
            "ctx": ctx,
            "tp": lax.rem(tp + step // CORES, n_tp),
            "dp": dp - core + lax.rem(core + step % CORES, CORES),
        }

    def farthest_first(outer, inner):
        def hops(step):
            far, near = step // inner, step % inner
            return min(far, outer - far) + min(near, inner - near)

        return sorted(range(1, outer * inner), key=lambda step: -hops(step))

    ring_steps = farthest_first(ring, SIDE)
    tp_steps = farthest_first(n_tp, CORES)

    barrier = pltpu.get_barrier_semaphore()
    partners = [along_ring_x(step) for step in ring_steps] + [
        along_tp_core(step) for step in tp_steps
    ]
    for partner in partners:
        pl.semaphore_signal(barrier, inc=1, device_id=partner, device_id_type=MESH)

    loads = [
        pltpu.make_async_copy(src, dst, load_sem.at[index])
        for index, (src, dst) in enumerate(
            (
                (q_gain_hbm, q_gain_ref),
                (k_gain_hbm, k_gain_ref),
                (k_hbm, k_raw.at[0]),
                (q_hbm, q_raw.at[0]),
                (v_hbm, v_all.at[0]),
                (o_hbm, o_all.at[0]),
            )
        )
    ]
    for one in loads:
        one.start()

    count = [0]
    started = []

    def copy(src, dst, device):
        index = count[0]
        count[0] += 1
        one = pltpu.make_async_remote_copy(
            src_ref=src,
            dst_ref=dst,
            send_sem=send_sem.at[index],
            recv_sem=recv_sem.at[index],
            device_id=device,
            device_id_type=MESH,
        )
        started.append(one)
        return one

    def cols(head):
        return slice(head * width, (head + 1) * width)

    pl.semaphore_wait(barrier, len(partners))

    halves = [pl.ds(0, rows // 2), pl.ds(rows // 2, rows // 2)]
    q_up = [copy(q_hbm.at[half], q_raw.at[1, half], along_z(1)) for half in halves]
    q_down = copy(q_hbm, q_raw.at[3], along_z(3))
    o_up = copy(o_hbm, o_all.at[1], along_z(1))
    o_down = [copy(o_hbm.at[half], o_all.at[3, half], along_z(3)) for half in halves]
    k_up = copy(k_hbm, k_raw.at[1], along_x(1))
    k_down = copy(k_hbm, k_raw.at[3], along_x(3))
    v_up = copy(v_hbm, v_all.at[1], along_x(1))
    v_down = copy(v_hbm, v_all.at[3], along_x(3))
    first = (q_up[0], o_down[0], q_up[1], o_down[1])
    for one in first + (k_up, v_down, o_up, q_down, v_up, k_down):
        one.start()
    q_far = [copy(q_raw.at[1, half], q_raw.at[2, half], along_z(1)) for half in halves]
    o_far = [copy(o_all.at[3, half], o_all.at[2, half], along_z(3)) for half in halves]
    k_far = copy(k_raw.at[1], k_raw.at[2], along_x(1))
    v_far = copy(v_all.at[3], v_all.at[2], along_x(3))

    stat_own[...] = jnp.zeros_like(stat_own)
    for one in loads:
        one.wait()

    def norm_q(slot):
        for head in range(heads):
            values = q_raw[slot, :, cols(head)].astype(jnp.float32)
            inverse = lax.rsqrt(jnp.mean(values * values, axis=1, keepdims=True) + EPSILON)
            unit = values * inverse
            q_unit[slot, :, cols(head)] = unit
            q_normed[slot, :, cols(head)] = (unit * q_gain_ref[...]).astype(jnp.bfloat16)
            if slot == 0:
                q_inverse[:, cols(head)] = jnp.broadcast_to(inverse, (rows, width))

    def norm_k(slot):
        here = slice(slot * rows, (slot + 1) * rows)
        for head in range(heads):
            values = k_raw[slot, :, cols(head)].astype(jnp.float32)
            inverse = lax.rsqrt(jnp.mean(values * values, axis=1, keepdims=True) + EPSILON)
            unit = values * inverse
            normed = (unit * k_gain_ref[...]).astype(jnp.bfloat16)
            k_unit[here, cols(head)] = unit
            k_normed[here, cols(head)] = normed
            k_turned[head, :, here] = normed.T
            if slot == 0:
                k_inverse[:, cols(head)] = jnp.broadcast_to(inverse, (rows, width))

    norm_q(0)
    norm_k(0)

    k_up.wait_recv()
    k_far.start()
    v_down.wait_recv()
    v_far.start()
    norm_k(1)
    k_down.wait_recv()
    norm_k(3)
    v_up.wait_recv()
    for half in range(2):
        q_up[half].wait_recv()
        q_far[half].start()
        o_down[half].wait_recv()
        o_far[half].start()
    k_far.wait_recv()
    norm_k(2)
    v_far.wait_recv()

    def contract_last(left, right):
        return lax.dot_general(
            left, right, (((1,), (1,)), ((), ())), preferred_element_type=jnp.float32
        )

    stat_copies = {}

    def first_pass(slot):
        for head in range(heads):
            scores = (
                contract_last(k_normed[:, cols(head)], q_normed[slot, :, cols(head)]) * scale
            )
            top = jnp.max(scores, axis=0, keepdims=True)
            weights = jnp.exp(scores - top)
            slopes = contract_last(
                v_all[:, :, cols(head)].reshape(keys, width), o_all[slot, :, cols(head)]
            )
            expo[slot, head] = weights
            dprob[slot, head] = slopes * scale
            stat_own[slot, 3 * head : 3 * head + 1] = top
            stat_own[slot, 3 * head + 1 : 3 * head + 2] = jnp.sum(weights, axis=0, keepdims=True)
            stat_own[slot, 3 * head + 2 : 3 * head + 3] = jnp.sum(
                weights * slopes, axis=0, keepdims=True
            )
        for step in (2, 1, 3):
            there = (slot + step) % SIDE
            one = copy(stat_own.at[slot], stat_in.at[there, step], along_z(step))
            stat_copies[there, step] = one
            one.start()

    first_pass(0)
    o_up.wait_recv()
    norm_q(1)
    first_pass(1)
    q_down.wait_recv()
    norm_q(3)
    first_pass(3)
    for one in q_far:
        one.wait_recv()
    norm_q(2)
    for one in o_far:
        one.wait_recv()
    first_pass(2)

    def second_pass(slot):
        for step in range(1, SIDE):
            stat_copies[slot, step].wait_recv()
        part = jnp.zeros((1, width), jnp.float32)
        for head in range(heads):
            tops = [stat_own[slot, 3 * head : 3 * head + 1]]
            totals = [stat_own[slot, 3 * head + 1 : 3 * head + 2]]
            weighted = [stat_own[slot, 3 * head + 2 : 3 * head + 3]]
            for step in range(1, SIDE):
                tops.append(stat_in[slot, step, 3 * head : 3 * head + 1])
                totals.append(stat_in[slot, step, 3 * head + 1 : 3 * head + 2])
                weighted.append(stat_in[slot, step, 3 * head + 2 : 3 * head + 3])
            top = functools.reduce(jnp.maximum, tops)
            factors = [jnp.exp(one - top) for one in tops]
            total = sum(one * factor for one, factor in zip(totals, factors))
            delta = sum(one * factor for one, factor in zip(weighted, factors)) / total
            prob = expo[slot, head] * (factors[0] / total)
            dscore = (prob * (dprob[slot, head] - delta * scale)).astype(jnp.bfloat16)
            prob_low = prob.astype(jnp.bfloat16)
            dq = jnp.dot(k_turned[head], dscore, preferred_element_type=jnp.float32).T
            part += jnp.sum(dq * q_unit[slot, :, cols(head)], axis=0, keepdims=True)
            dq_full[slot, head] = dq
            dk = jnp.dot(
                dscore, q_normed[slot, :, cols(head)], preferred_element_type=jnp.float32
            )
            dv = jnp.dot(
                prob_low, o_all[slot, :, cols(head)], preferred_element_type=jnp.float32
            )
            if slot == 2:
                dk_acc[:, cols(head)] = dk
                dv_acc[:, cols(head)] = dv
            else:
                dk_acc[:, cols(head)] += dk
                dv_acc[:, cols(head)] += dv
        return part

    def via(head):
        return 1 if head % 2 == 0 else 3

    def start(src, dst, device):
        one = copy(src, dst, device)
        one.start()
        return one

    dq_far_copies, dq_copies = [], []
    q_gain_part = second_pass(2)
    for head in range(heads):
        dq_send[2, head] = dq_full[2, head].astype(jnp.bfloat16)
        device = along_z(SIDE - via(head))
        dq_far_copies.append(start(dq_send.at[2, head], dq_far.at[head], device))
    for slot in (1, 3):
        q_gain_part += second_pass(slot)
        for head in range(heads):
            if via(head) != slot:
                dq_send[slot, head] = dq_full[slot, head].astype(jnp.bfloat16)
                device = along_z(SIDE - slot)
                dq_copies.append(start(dq_send.at[slot, head], dq_in.at[slot, head], device))
    q_gain_part += second_pass(0)

    def block(slot):
        return slice(slot * rows, (slot + 1) * rows)

    k_gain_part = jnp.zeros((1, width), jnp.float32)
    for head in range(heads):
        k_gain_part += jnp.sum(
            dk_acc[:, cols(head)] * k_unit[:, cols(head)], axis=0, keepdims=True
        )
    part = jnp.concatenate([q_gain_part, k_gain_part], axis=0)

    def spread(buffer, steps, place, device, part):
        buffer[place] = part
        return [start(buffer.at[place], buffer.at[place], device(step)) for step in steps]

    def gathered(buffer, copies):
        for one in copies:
            one.wait_recv()
        part = buffer[0]
        for index in range(1, len(copies) + 1):
            part += buffer[index]
        return part

    gain_copies = spread(gain_tp, tp_steps, tp * CORES + core, along_tp_core, part)

    dk_send[2] = dk_acc[block(2), :].astype(jnp.bfloat16)
    dk_far_copy = start(dk_send.at[2], dk_far, along_x(3))
    dv_send[2] = dv_acc[block(2), :].astype(jnp.bfloat16)
    dv_far_copy = start(dv_send.at[2], dv_far, along_x(1))
    dk_send[3] = dk_acc[block(3), :].astype(jnp.bfloat16)
    dk_near = start(dk_send.at[3], dk_in.at[3], along_x(1))
    dv_send[1] = dv_acc[block(1), :].astype(jnp.bfloat16)
    dv_near = start(dv_send.at[1], dv_in.at[1], along_x(3))

    for head in range(heads):
        slot = via(head)
        dq_far_copies[head].wait_recv()
        total = dq_full[slot, head] + dq_far[head].astype(jnp.float32)
        dq_send[slot, head] = total.astype(jnp.bfloat16)
        device = along_z(SIDE - slot)
        dq_copies.append(start(dq_send.at[slot, head], dq_in.at[slot, head], device))

    dk_far_copy.wait_recv()
    total = dk_acc[block(1), :] + dk_far[...].astype(jnp.float32)
    dk_send[1] = total.astype(jnp.bfloat16)
    dk_last = start(dk_send.at[1], dk_in.at[1], along_x(3))
    dv_far_copy.wait_recv()
    total = dv_acc[block(3), :] + dv_far[...].astype(jnp.float32)
    dv_send[3] = total.astype(jnp.bfloat16)
    dv_last = start(dv_send.at[3], dv_in.at[3], along_x(1))

    part = gathered(gain_tp, gain_copies)
    gain_copies = spread(gain_z, ring_steps, z_place * SIDE + x, along_ring_x, part)

    def restore(grad, unit, inverse, gain):
        scaled = grad * gain
        return inverse * (scaled - unit * jnp.mean(scaled * unit, axis=1, keepdims=True))

    for one in dq_copies:
        one.wait_recv()
    for head in range(heads):
        grad = dq_full[0, head]
        for slot in (1, 3):
            grad += dq_in[slot, head].astype(jnp.float32)
        grad_out[0, :, cols(head)] = restore(
            grad, q_unit[0, :, cols(head)], q_inverse[:, cols(head)], q_gain_ref[...]
        ).astype(jnp.bfloat16)

    for one in (dk_near, dv_near, dk_last, dv_last):
        one.wait_recv()
    for head in range(heads):
        grad = dk_acc[block(0), cols(head)]
        total = dv_acc[block(0), cols(head)]
        for slot in (1, 3):
            grad += dk_in[slot, :, cols(head)].astype(jnp.float32)
            total += dv_in[slot, :, cols(head)].astype(jnp.float32)
        grad_out[1, :, cols(head)] = restore(
            grad, k_unit[block(0), cols(head)], k_inverse[:, cols(head)], k_gain_ref[...]
        ).astype(jnp.bfloat16)
        grad_out[2, :, cols(head)] = total.astype(jnp.bfloat16)

    gain_out[...] = gathered(gain_z, gain_copies) / length
    for one in started:
        one.wait_send()


def deliver(grad_in, gain_in, dq_out, dk_out, dv_out, q_gain_out, k_gain_out, sem):
    pairs = (
        (grad_in.at[0], dq_out.at[0]),
        (grad_in.at[1], dk_out.at[0]),
        (grad_in.at[2], dv_out.at[0]),
    )
    copies = [pltpu.make_async_copy(a, b, sem.at[i]) for i, (a, b) in enumerate(pairs)]
    for one in copies:
        one.start()
    q_gain_out[...] = gain_in[0:1]
    k_gain_out[...] = gain_in[1:2]
    for one in copies:
        one.wait()


def local(q_raw, k_raw, value, d_out, q_gain, k_gain):
    width = q_gain.shape[0]
    rows, flat = q_raw.shape[1:]
    heads = flat // width
    n_ctx, n_tp, n_dp = (lax.axis_size(name) for name in ("ctx", "tp", "dp"))
    keys = SIDE * rows
    low, full = jnp.bfloat16, jnp.float32
    copies = 16 + 12 + 3 * heads + 6 + SIDE * SIDE * n_dp // CORES - 1 + n_tp * CORES - 1
    sizes = (n_tp, n_dp, heads, n_ctx * rows)
    block = jax.ShapeDtypeStruct((3, rows, flat), low)
    vmem = pl.BlockSpec(memory_space=pltpu.VMEM)
    grads, gains = pl.pallas_call(
        functools.partial(kernel, sizes),
        out_shape=(block, jax.ShapeDtypeStruct((2, width), full)),
        in_specs=[pl.BlockSpec(memory_space=pl.ANY)] * 6,
        out_specs=(vmem,) * 2,
        scratch_shapes=[
            pltpu.VMEM((1, width), full),
            pltpu.VMEM((1, width), full),
            pltpu.VMEM((SIDE, rows, flat), low),
            pltpu.VMEM((SIDE, rows, flat), low),
            pltpu.VMEM((SIDE, rows, flat), low),
            pltpu.VMEM((SIDE, rows, flat), low),
            pltpu.VMEM((SIDE, rows, flat), low),
            pltpu.VMEM((SIDE, rows, flat), full),
            pltpu.VMEM((rows, flat), full),
            pltpu.VMEM((keys, flat), low),
            pltpu.VMEM((keys, flat), full),
            pltpu.VMEM((rows, flat), full),
            pltpu.VMEM((heads, width, keys), low),
            pltpu.VMEM((SIDE, heads, keys, rows), full),
            pltpu.VMEM((SIDE, heads, keys, rows), full),
            pltpu.VMEM((SIDE, 8, rows), full),
            pltpu.VMEM((SIDE, SIDE, 8, rows), full),
            pltpu.VMEM((keys, flat), full),
            pltpu.VMEM((keys, flat), full),
            pltpu.VMEM((SIDE, rows, flat), low),
            pltpu.VMEM((SIDE, rows, flat), low),
            pltpu.VMEM((SIDE, rows, flat), low),
            pltpu.VMEM((SIDE, rows, flat), low),
            pltpu.VMEM((rows, flat), low),
            pltpu.VMEM((rows, flat), low),
            pltpu.VMEM((SIDE, heads, rows, width), full),
            pltpu.VMEM((SIDE, heads, rows, width), low),
            pltpu.VMEM((SIDE, heads, rows, width), low),
            pltpu.VMEM((heads, rows, width), low),
            pltpu.VMEM((n_tp * CORES, 2, width), full),
            pltpu.VMEM((SIDE * SIDE * n_dp // CORES, 2, width), full),
            pltpu.SemaphoreType.DMA((6,)),
            pltpu.SemaphoreType.DMA((copies,)),
            pltpu.SemaphoreType.DMA((copies,)),
        ],
        compiler_params=pltpu.CompilerParams(collective_id=0, has_side_effects=True),
    )(
        q_raw[0],
        k_raw[0],
        value[0],
        d_out[0],
        q_gain[None],
        k_gain[None],
    )
    one = jax.ShapeDtypeStruct((1, rows, flat), low)
    line = jax.ShapeDtypeStruct((1, width), full)
    hbm = pl.BlockSpec(memory_space=pl.ANY)
    dq, dk, dv, q_part, k_part = pl.pallas_call(
        deliver,
        out_shape=(one, one, one, line, line),
        in_specs=[vmem, vmem],
        out_specs=(hbm, hbm, hbm, vmem, vmem),
        scratch_shapes=[pltpu.SemaphoreType.DMA((3,))],
    )(grads, gains)
    return (dq, dk, dv, q_part[0], k_part[0])


def solution(mesh):
    split = P("dp", "ctx", "tp")
    return jax.shard_map(
        local,
        mesh=mesh,
        in_specs=(split, split, split, split, P(), P()),
        out_specs=(split, split, split, P(), P()),
        check_vma=False,
    )
```
